32 devices in a mesh: seq: 8 (over z, x), tensor: 4 (over y, core).
Axes of the slice: x: 2, y: 2, z: 4, core: 2. Of those that a mesh axis runs over, the one named last changes fastest.
Arguments:
- latents: bfloat16 [1024, 2560], P('seq'), may hold values from -6 to 6
- levels: int32 [8], P('seq'), may hold values from 0 to 999
- head_slot: int32 [1], replicated, may hold values from 0 to 7
- fresh_noise: bfloat16 [128, 2560], P(None, 'tensor'), may hold values from -6 to 6
- ada_weight: bfloat16 [256, 3, 2560], P(None, None, 'tensor'), may hold values from -0.375 to 0.375
- qkv_weight: bfloat16 [2560, 3, 1536], P(None, None, 'tensor'), may hold values from -0.125 to 0.125
- q_gain: float32 [128], replicated, may hold values from 0.5 to 2.5
- k_gain: float32 [128], replicated, may hold values from 0.5 to 2.5
- out_weight: bfloat16 [1536, 2560], P('tensor'), may hold values from -0.15625 to 0.15625
Outputs:
- window: bfloat16 [1024, 2560], P('seq', 'tensor')
- clean: bfloat16 [128, 2560], P('seq', 'tensor')
The draws below stay inside these ranges and needn't reach their ends.
All inputs are finite; a program needn't handle non-finite values.
Results may differ from the reference program's by a relative error of at most 0.0053.
Values may be sent and summed in bfloat16 or wider, within the bound.
A program may use at most 64 MiB of HBM per device.

```python
import math
import jax
import jax.numpy as jnp
from jax import lax

D = 2560
HEADS = 12
HD = 128
TEMB = 256
LEVELS = 1000
GROUP = 128
GROUPS = 8
FRAMES = 1024


def set_ends(drawn, rng, least, high):
    dims = drawn.shape
    place = [jax.random.randint(jax.random.fold_in(rng, axis), (), 0, dims[axis]) for axis in range(len(dims))]
    drawn = drawn.at[tuple(place)].set(least)
    longest = dims.index(max(dims))
    place[longest] = (place[longest] + 1) % dims[longest]
    return drawn.at[tuple(place)].set(high)


def block_levels(key, dims, cuts, least, top_value):
    loudness, own = 1.0, jax.random.fold_in(key, 6)
    for position, shards_of in cuts:
        draws = jnp.exp(jax.random.uniform(jax.random.fold_in(own, position), (shards_of,), jnp.float32, least / len(cuts), top_value / len(cuts)))
        loudness = loudness * jnp.repeat(draws, dims[position] // shards_of).reshape([-1 if axis == position else 1 for axis in range(len(dims))])
    return loudness


def noise(key, shape, scale, limit, cuts=(), held_as=jnp.bfloat16):
    factor_of = block_levels(key, shape, cuts, -0.22, 0.18) if cuts else 1.0
    array = jax.random.normal(key, shape, jnp.float32) * scale * factor_of
    return jnp.minimum(jnp.maximum(array, -limit), limit).astype(held_as)


def setup_inputs(seed: int = 0) -> dict:
    splits = jax.random.split(jax.random.key(seed), 10)
    return {
        "latents": noise(splits[0], (FRAMES, D), 1.0, 6.0, ((0, 8),)),
        "levels": set_ends(jax.random.randint(splits[1], (GROUPS,), 0, LEVELS), jax.random.fold_in(splits[1], 1), 0, LEVELS - 1).astype(jnp.int32),
        "head_slot": jax.random.randint(splits[2], (1,), 0, GROUPS).astype(jnp.int32),
        "fresh_noise": noise(splits[3], (GROUP, D), 1.0, 6.0, ((1, 4),)),
        "ada_weight": noise(splits[4], (TEMB, 3, D), TEMB ** -0.5, 0.375, ((2, 4),)),
        "qkv_weight": noise(splits[5], (D, 3, HEADS * HD), D ** -0.5, 0.125, ((2, 4),)),
        "q_gain": jnp.clip(jnp.exp(jax.random.uniform(splits[6], (HD,), jnp.float32, math.log(0.5), math.log(2.5))), 0.5, 2.5),
        "k_gain": jnp.clip(jnp.exp(jax.random.uniform(splits[7], (HD,), jnp.float32, math.log(0.5), math.log(2.5))), 0.5, 2.5),
        "out_weight": noise(splits[8], (HEADS * HD, D), (HEADS * HD) ** -0.5, 0.15625, ((0, 4),)),
    }


def modulation(levels, ada_weight):
    half_width = TEMB // 2
    frequency = jnp.exp(-math.log(10000.0) * jnp.arange(half_width, dtype=jnp.float32) / half_width)
    angles = levels.astype(jnp.float32)[:, None] * frequency[None, :]
    embedding = jax.nn.silu(jnp.concatenate([jnp.cos(angles), jnp.sin(angles)], axis=1)).astype(jnp.bfloat16)
    flat = jnp.dot(embedding, ada_weight.reshape(TEMB, 3 * D), preferred_element_type=jnp.float32)
    return flat.reshape(-1, 3, D)

def modulate(states, offset_terms, scale_terms):
    average = lax.optimization_barrier(jnp.mean(states, axis=-1, keepdims=True))
    centered = states - average
    variance = lax.optimization_barrier(jnp.mean(centered * centered, axis=-1, keepdims=True))
    normed = centered * lax.rsqrt(variance + 1e-06)
    return (normed * (1.0 + scale_terms) + offset_terms).astype(jnp.bfloat16)

def rms_scaled(matrix, gain_vector, factor):
    power = lax.optimization_barrier(jnp.mean(matrix * matrix, axis=-1, keepdims=True))
    return (matrix * lax.rsqrt(power + 1e-06) * gain_vector * factor).astype(jnp.bfloat16)

def project(hidden, qkv_weight, q_gain, k_gain):
    projected_all = jnp.dot(hidden, qkv_weight.reshape(D, 3 * HEADS * HD), preferred_element_type=jnp.float32)
    projected_all = projected_all.reshape(-1, 3, HEADS, HD)
    queries = rms_scaled(projected_all[:, 0], q_gain, 1.0 / math.sqrt(HD))
    keys = rms_scaled(projected_all[:, 1], k_gain, 1.0)
    values = projected_all[:, 2].astype(jnp.bfloat16)
    return (queries, keys, values)

def reference(latents, levels, head_slot, fresh_noise, ada_weight, qkv_weight, q_gain, k_gain, out_weight):
    oldest = head_slot[0].astype(jnp.int32)
    modulations = modulation(levels, ada_weight)
    states = latents.astype(jnp.float32).reshape(GROUPS, GROUP, D)
    hidden = modulate(states, modulations[:, 0][:, None], modulations[:, 1][:, None]).reshape(GROUPS * GROUP, D)
    queries, keys, values = project(hidden, qkv_weight, q_gain, k_gain)
    query_blocks = queries.reshape(GROUPS, GROUP, HEADS, HD)
    key_blocks = keys.reshape(GROUPS, GROUP, HEADS, HD)
    value_blocks = values.reshape(GROUPS, GROUP, HEADS, HD)
    block_ranks = (jnp.arange(GROUPS, dtype=jnp.int32) - oldest) % GROUPS

    def one_block(query_index):
        query_tile = query_blocks[query_index].astype(jnp.float32)
        initial = (jnp.zeros((HEADS, GROUP), jnp.float32), jnp.zeros((GROUP, HEADS, HD), jnp.float32))

        def absorb(state_now, key_index):

            def update_state(state_old):
                running_sum, weighted = state_old
                key_tile = key_blocks[key_index].astype(jnp.float32)
                value_tile = value_blocks[key_index].astype(jnp.float32)
                scores = jnp.einsum('qhd,khd->hqk', query_tile, key_tile)
                weights = jnp.exp(scores)
                running_sum = running_sum + lax.optimization_barrier(jnp.sum(weights, axis=-1))
                rounded = lax.optimization_barrier(weights.astype(jnp.bfloat16)).astype(jnp.float32)
                weighted = weighted + jnp.einsum('hqk,khd->qhd', rounded, value_tile)
                return (running_sum, weighted)

            def keep_state(state_old):
                return state_old
            visible = block_ranks[key_index] <= block_ranks[query_index]
            return (lax.cond(visible, update_state, keep_state, state_now), None)
        finished, unused = lax.scan(absorb, initial, jnp.arange(GROUPS, dtype=jnp.int32))
        return (finished[1] / finished[0].T[..., None]).astype(jnp.bfloat16)
    attended = lax.map(one_block, jnp.arange(GROUPS, dtype=jnp.int32)).reshape(GROUPS * GROUP, HEADS * HD)
    projected = jnp.dot(attended, out_weight, preferred_element_type=jnp.float32).reshape(GROUPS, GROUP, D)
    updated = (states + modulations[:, 2][:, None] * projected).astype(jnp.bfloat16)
    clean = lax.dynamic_index_in_dim(updated, oldest, 0, keepdims=False)
    leaving = (block_ranks == 0)[:, None, None]
    window = jnp.where(leaving, fresh_noise[None], updated).reshape(GROUPS * GROUP, D)
    return (window, clean)
```

```python
import functools
import math

import jax
import jax.numpy as jnp
from jax import lax
from jax.experimental import pallas as pl
from jax.experimental.pallas import tpu as pltpu
from jax.sharding import PartitionSpec as P

F32 = jnp.float32
BF16 = jnp.bfloat16
EPS = 1e-06


def dot(a, b):
    return jnp.dot(a, b, preferred_element_type=F32)


def dot_t(a, b):
    return lax.dot_general(a, b, (((1,), (1,)), ((), ())), preferred_element_type=F32)


def kernel(
    n, parts, slab, clean_rows,
    head_hbm, level_hbm, q_gain_hbm, k_gain_hbm, noise_hbm, lat_hbm, ada_hbm, qkv_hbm, out_hbm,
    updated_ref,
    head_ref, level_ref, q_gain_ref, k_gain_ref, noise, lat, ada, wqkv, wout, normed, mods, gates,
    lat_rows, raw, stage, queries, kv, acc, totals, result, attended,
    load_sem, mod_send, mod_recv, gate_send, gate_recv, row_send, row_recv, w_send, w_recv,
    q_send, q_recv, kv_send, kv_recv, relay_send, back_send, att_recv, sib_send, cross_send,
):
    me = lax.axis_index("seq")
    part = lax.axis_index("tensor")
    pair = 2
    core = lax.rem(part, pair)
    plane = part // pair
    planes = parts // pair
    sibling = plane * pair + 1 - core
    rows, width = lat.shape
    columns = updated_ref.shape[1]
    head_size = q_gain_ref.shape[1]
    heads = stage.shape[1]
    half = rows // pair
    piece = half + slab
    owners = heads * pair
    first = (n - owners) // 2
    mine = me - first
    active = (mine >= 0) & (mine < owners)
    own_head = jnp.clip(mine // pair, 0, heads - 1)
    own_core = lax.rem(mine + owners * n, pair)

    def remote(src, dst, send, recv, target):
        return pltpu.make_async_remote_copy(
            src_ref=src, dst_ref=dst, send_sem=send, recv_sem=recv,
            device_id=target, device_id_type=pl.DeviceIdType.MESH,
        )

    def at_core(seq, which):
        return {"seq": seq, "tensor": plane * pair + which}

    loads = [
        pltpu.make_async_copy(ada_hbm, ada, load_sem.at[0]),
        pltpu.make_async_copy(lat_hbm, lat, load_sem.at[1]),
        pltpu.make_async_copy(qkv_hbm.at[0], wqkv.at[0], load_sem.at[2]),
        pltpu.make_async_copy(qkv_hbm.at[1], wqkv.at[1], load_sem.at[3]),
        pltpu.make_async_copy(qkv_hbm.at[2], wqkv.at[2], load_sem.at[4]),
        pltpu.make_async_copy(
            out_hbm.at[:, pl.ds(pl.multiple_of(part * columns, 128), columns)],
            wout.at[part], load_sem.at[5],
        ),
        pltpu.make_async_copy(noise_hbm, noise, load_sem.at[6]),
    ]
    small = [
        pltpu.make_async_copy(source, held, load_sem.at[7 + index])
        for index, (source, held) in enumerate((
            (level_hbm, level_ref), (head_hbm, head_ref),
            (q_gain_hbm, q_gain_ref), (k_gain_hbm, k_gain_ref),
        ))
    ]
    for load in small:
        load.start()
    for load in loads:
        load.start()

    barrier = pltpu.get_barrier_semaphore()
    for step in range(1, planes):
        for which in range(pair):
            pl.semaphore_signal(
                barrier, inc=1,
                device_id={"tensor": lax.rem(plane + step, planes) * pair + which},
                device_id_type=pl.DeviceIdType.MESH,
            )
    pl.semaphore_signal(
        barrier, inc=1, device_id={"tensor": sibling}, device_id_type=pl.DeviceIdType.MESH
    )

    @pl.loop(1, n)
    def _(step):
        for which in range(pair):
            pl.semaphore_signal(
                barrier, inc=1, device_id=at_core(lax.rem(me + step, n), which),
                device_id_type=pl.DeviceIdType.MESH,
            )

    for load in small:
        load.wait()
    half_width = ada.shape[1] // 2
    order = lax.broadcasted_iota(jnp.int32, (16, half_width), 1).astype(F32)
    angles = level_ref[0].astype(F32) * jnp.exp(-math.log(10000.0) * order / half_width)
    waves = jnp.concatenate([jnp.cos(angles), jnp.sin(angles)], axis=1)
    emb = (waves * (1.0 / (1.0 + jnp.exp(-waves)))).astype(BF16)
    loads[0].wait()
    for j in range(2):
        mods[part, j : j + 1, :] = dot(emb, ada[j])[0:1]
    gates[me] = dot(emb, ada[2])[0:1]

    pl.semaphore_wait(barrier, pair * n - 1 + parts - pair)

    def mod_copy(slot, target):
        return remote(
            mods.at[slot], mods.at[slot], mod_send.at[target], mod_recv.at[slot],
            {"tensor": target},
        )

    for step in range(1, parts):
        mod_copy(part, lax.rem(part + step, parts)).start()

    def slab_of(device):
        return pl.multiple_of((device * clean_rows) // slab * slab, slab)

    first_column = pl.multiple_of(part * columns, 128)

    def gate_copy(slot, target):
        return remote(
            gates.at[slot], gates.at[slot], gate_send.at[target], gate_recv.at[slot],
            {"seq": target},
        )

    def row_copy(slot, target):
        return remote(
            lat_hbm.at[pl.ds(slab_of(target), slab), pl.ds(first_column, columns)],
            lat_rows.at[slot], row_send.at[target], row_recv.at[slot], {"seq": target},
        )

    def w_copy(slot, target):
        at = pl.ds(pl.multiple_of(target * columns, 128), columns)
        return remote(
            out_hbm.at[:, at], wout.at[slot], w_send.at[target], w_recv.at[slot],
            {"tensor": target},
        )

    @pl.loop(1, n)
    def _(step):
        target = lax.rem(me + step, n)
        gate_copy(me, target).start()
        row_copy(me, target).start()

    for step in range(1, parts):
        w_copy(part, lax.rem(part + step, parts)).start()

    loads[1].wait()
    own_slab = slab_of(me)
    lat_rows[me] = lat[pl.ds(own_slab, slab), pl.ds(first_column, columns)]

    tile = 16

    @pl.loop(0, rows // tile, unroll=4)
    def _(index):
        at = pl.ds(pl.multiple_of(index * tile, tile), tile)
        states = lat[at, :].astype(F32)
        centered = states - jnp.mean(states, axis=-1, keepdims=True)
        variance = jnp.mean(centered * centered, axis=-1, keepdims=True)
        scaled_rows = centered * lax.rsqrt(variance + EPS)
        for index in range(parts):
            normed[index, at, :] = scaled_rows[:, index * columns : (index + 1) * columns]

    def hidden_of(slot):
        return (normed[slot] * (1.0 + mods[slot, 1:2, :]) + mods[slot, 0:1, :]).astype(BF16)

    own_hidden = hidden_of(part)
    for kind in range(3):
        loads[2 + kind].wait()
        raw[kind] = dot(own_hidden, wqkv[kind, part])
    mod_copy(sibling, part).wait_recv()
    sib_hidden = hidden_of(sibling)
    for kind in range(3):
        raw[kind] += dot(sib_hidden, wqkv[kind, sibling])

    others = [
        lax.rem(plane + step, planes) * pair + which
        for step in range(1, planes) for which in range(pair)
    ]
    for slot in others:
        mod_copy(slot, part).wait_recv()
    rest = [hidden_of(slot) for slot in others]

    def whole(kind):
        total = raw[kind]
        for hidden, slot in zip(rest, others):
            total = total + dot(hidden, wqkv[kind, slot])
        return total

    def scaled(matrix, gain, factor):
        power = jnp.mean(matrix * matrix, axis=-1, keepdims=True)
        return (matrix * lax.rsqrt(power + EPS) * gain * factor).astype(BF16)

    def head_at(index):
        return slice(index * head_size, (index + 1) * head_size)

    def turn(step):
        return jnp.where(me < n // 2, heads - 1 - step, step)

    def owner_of(h):
        return first + pair * h + core

    def q_copy(h, which, source):
        return remote(
            stage.at[0, h, pl.ds(pl.multiple_of(which * half, half), half)], queries.at[source],
            q_send.at[h, which], q_recv.at[source], at_core(owner_of(h), which),
        )

    def kv_copy(kind, h, source, which):
        return remote(
            stage.at[1 + kind, h], kv.at[kind, source], kv_send.at[kind, h],
            kv_recv.at[kind, source], at_core(owner_of(h), which),
        )

    def q_each(act):
        for step in range(heads):
            h = turn(step)
            for which in range(pair):

                @pl.when((owner_of(h) != me) | (core != which))
                def _():
                    act(q_copy(h, which, me))

    def kv_each(kind, act):
        for step in range(heads):
            h = turn(step)
            which = jnp.where(owner_of(h) == me, 1 - core, lax.rem(me, pair))
            act(kv_copy(kind, h, me, which))

    value = whole(0)
    for h in range(heads):
        stage[0, h] = scaled(value[:, head_at(h)], q_gain_ref[...], 1.0 / math.sqrt(head_size))
    q_each(lambda copy: copy.start())
    value = whole(1)
    for h in range(heads):
        stage[1, h] = scaled(value[:, head_at(h)], k_gain_ref[...], 1.0)
    kv_each(0, lambda copy: copy.start())
    value = whole(2)
    for h in range(heads):
        stage[2, h] = value[:, head_at(h)].astype(BF16)
    kv_each(1, lambda copy: copy.start())

    oldest = head_ref[0]

    def rank_of(block):
        return lax.rem(block - oldest + n, n)

    local_kv = active & (own_core == core)

    def relay(kind, source):
        return remote(
            kv.at[kind, source], kv.at[kind, source], relay_send.at[kind, source],
            kv_recv.at[kind, source], {"tensor": sibling},
        )

    def take(kind, source):
        @pl.when((source != me) | (own_core != core))
        def _():
            kv_copy(kind, 0, source, core).wait_recv()

    line = n // pair
    lane = lax.rem(me, pair)
    spot = me // pair

    def nearby(step, column):
        away = (step + 1) // 2 * (1 - 2 * lax.rem(step + 1, 2))
        return lax.rem(spot + away + n, line) * pair + column

    group = min(n, 8)

    def absorb(source):
        rank = rank_of(source)

        def some(base):
            at = pl.ds(base, group)
            q = queries[at].reshape(group * half, head_size)
            weights = jnp.exp(dot_t(q, kv[0, source])).reshape(group, half, head_size)
            weights = jnp.concatenate([
                jnp.where(
                    jnp.full((1, half, head_size), rank, jnp.int32) <= rank_of(base + index),
                    weights[index : index + 1], 0.0,
                )
                for index in range(group)
            ], axis=0)
            totals[at] += weights
            product = dot(
                weights.astype(BF16).reshape(group * half, head_size), kv[1, source]
            )
            acc[at] += product.reshape(group, half, head_size)

        if n == group:
            some(0)
        else:
            pl.loop(0, n // group)(lambda index: some(index * group))

    slot_at = plane * pair + own_core

    def back_copy(target):
        return remote(
            result.at[target],
            attended.at[slot_at, own_head, pl.ds(pl.multiple_of(core * piece, 16), piece)],
            back_send.at[target], att_recv.at[slot_at, own_head, core], at_core(target, core),
        )

    def far_order(step):
        return jnp.where(me < n // 2, n - 1 - step, step)


    @pl.when(active)
    def _():
        acc[...] = jnp.zeros_like(acc)
        totals[...] = jnp.zeros_like(totals)

        @pl.when(own_core == core)
        def _():
            queries[me] = stage[0, own_head, pl.ds(pl.multiple_of(core * half, half), half)]
            for kind in range(2):
                kv[kind, me] = stage[1 + kind, own_head]

        @pl.loop(0, n)
        def _(source):
            @pl.when((source != me) | (own_core != core))
            def _():
                q_copy(0, core, source).wait_recv()


        @pl.loop(0, line)
        def _(step):
            source = nearby(step, core)
            take(0, source)

            @pl.when(source != me)
            def _():
                relay(0, source).start()


        @pl.loop(0, line)
        def _(step):
            source = nearby(step, core)
            take(1, source)

            @pl.when(source != me)
            def _():
                relay(1, source).start()

            absorb(source)


        @pl.loop(0, line)
        def _(step):
            source = nearby(step, 1 - core)
            take(0, source)
            take(1, source)
            absorb(source)


        @pl.loop(0, n, unroll=min(n, 8))
        def _(block):
            total = jnp.sum(totals[block], axis=-1, keepdims=True)
            result[block, 0:half] = (acc[block] / total).astype(BF16)

        @pl.loop(0, n, unroll=min(n, 8))
        def _(block):
            at = pl.multiple_of(lax.rem(slab_of(block), half), slab)
            result[block, half:] = result[oldest, pl.ds(at, slab), :]

        @pl.loop(0, n)
        def _(step):
            target = far_order(step)

            @pl.when(target != me)
            def _():
                back_copy(target).start()

        attended[slot_at, own_head, pl.ds(pl.multiple_of(core * piece, 16), piece)] = result[me]

    for step in range(1, parts):
        target = lax.rem(part + step, parts)
        mod_copy(part, target).wait_send()
    q_each(lambda copy: copy.wait_send())
    kv_each(0, lambda copy: copy.wait_send())
    kv_each(1, lambda copy: copy.wait_send())

    @pl.loop(1, n)
    def _(step):
        target = lax.rem(me + step, n)
        source = lax.rem(me - step + n, n)
        gate_copy(me, target).wait_send()
        row_copy(me, target).wait_send()
        gate_copy(source, me).wait_recv()
        row_copy(source, me).wait_recv()

    def region(slot, h, which):
        return attended.at[slot, h, pl.ds(pl.multiple_of(which * piece, 16), piece)]

    def arrival(slot, h, which):
        held = region(slot, h, which)
        return remote(
            held, held, sib_send.at[slot, h], att_recv.at[slot, h, which], {"tensor": sibling}
        )

    def across(slot, h, step):
        held = region(slot, h, core)
        return remote(
            held, held, cross_send.at[step - 1, slot, h], att_recv.at[slot, h, core],
            {"tensor": lax.rem(plane + step, planes) * pair + core},
        )

    def ordered(step):
        g = jnp.where(me < n // 2, step, owners - 1 - step)
        return g, plane * pair + lax.rem(g, pair), g // pair

    for step in range(owners):
        g, slot, h = ordered(step)

        @pl.when(first + g != me)
        def _():
            arrival(slot, h, core).wait_recv()

        for way in range(1, planes):
            across(slot, h, way).start()
        arrival(slot, h, core).start()

    def slot_dot(slot):
        w_rows = wout[slot]
        joined = jnp.concatenate([attended[slot, h] for h in range(heads)], axis=1)
        return dot(joined, w_rows)

    for way in range(1, planes):
        for step in range(owners):
            g, slot, h = ordered(step)
            slot = lax.rem(slot + way * pair, parts)
            arrival(slot, h, core).wait_recv()
            arrival(slot, h, core).start()

    loads[5].wait()
    total = None
    for which in range(pair):
        slot = plane * pair + which
        for h in range(heads):
            arrival(slot, h, 1 - core).wait_recv()
    w_copy(sibling, part).wait_recv()
    total = slot_dot(part) + slot_dot(sibling)
    for slot in others:
        w_copy(slot, part).wait_recv()
    for slot in others:
        for h in range(heads):
            arrival(slot, h, 1 - core).wait_recv()
        total = total + slot_dot(slot)

    own_rank = rank_of(me)
    own_states = lat[:, pl.ds(first_column, columns)].astype(F32)
    mixed = jnp.concatenate([total[0:half], total[piece : piece + half]], axis=0)
    updated = (own_states + gates[me] * mixed).astype(BF16)
    leaving = jnp.full((rows, columns), own_rank, jnp.int32) == 0
    loads[6].wait()
    updated_ref[0:rows, :] = jnp.where(leaving, noise[...], updated)
    upper = jnp.full((slab, columns), own_slab, jnp.int32) >= half
    clean = jnp.where(upper, total[piece + half :], total[half:piece])
    updated_ref[rows:, :] = (
        lat_rows[oldest].astype(F32) + gates[oldest] * clean
    ).astype(BF16)

    for step in range(1, parts):
        w_copy(part, lax.rem(part + step, parts)).wait_send()
    for slot in range(parts):
        for h in range(heads):
            arrival(slot, h, core).wait_send()
    for way in range(1, planes):
        for step in range(owners):
            g, slot, h = ordered(step)
            across(slot, h, way).wait_send()

    @pl.when(active)
    def _():
        @pl.loop(0, n)
        def _(target):
            @pl.when(target != me)
            def _():
                back_copy(target).wait_send()

        @pl.loop(0, line)
        def _(step):
            source = nearby(step, core)

            @pl.when(source != me)
            def _():
                relay(0, source).wait_send()
                relay(1, source).wait_send()


def finish_kernel(updated_ref, window_ref, clean_ref):
    rows = window_ref.shape[0]
    window_ref[...] = updated_ref[0:rows, :]
    clean_ref[...] = updated_ref[rows:, :]


def local(
    latents, levels, head_slot, fresh_noise, ada_weight, qkv_weight, q_gain, k_gain, out_weight
):
    n = lax.axis_size("seq")
    parts = lax.axis_size("tensor")
    rows, width = latents.shape
    columns = fresh_noise.shape[1]
    inner = out_weight.shape[0]
    clean_rows = rows // n
    slab = max(clean_rows, 16)
    heads = inner // q_gain.shape[0]
    head_size = q_gain.shape[0]
    half = rows // 2
    vmem = pl.BlockSpec(memory_space=pltpu.VMEM)
    hbm = pl.BlockSpec(memory_space=pltpu.HBM)
    dma = pltpu.SemaphoreType.DMA
    updated = pl.pallas_call(
        functools.partial(kernel, n, parts, slab, clean_rows),
        out_shape=pltpu.VMEM((rows + slab, columns), BF16),
        in_specs=[
            hbm, hbm, hbm, hbm, hbm, hbm, hbm, hbm, hbm,
        ],
        out_specs=vmem,
        scratch_shapes=[
            pltpu.SMEM((1,), jnp.int32),
            pltpu.SMEM((1,), jnp.int32),
            pltpu.VMEM((1, head_size), F32),
            pltpu.VMEM((1, head_size), F32),
            pltpu.VMEM((rows, columns), BF16),
            pltpu.VMEM((rows, width), BF16),
            pltpu.VMEM((3, ada_weight.shape[0], columns), BF16),
            pltpu.VMEM((3, parts, columns, inner), BF16),
            pltpu.VMEM((parts, inner, columns), BF16),
            pltpu.VMEM((parts, rows, columns), F32),
            pltpu.VMEM((parts, 8, columns), F32),
            pltpu.VMEM((n, 1, columns), F32),
            pltpu.VMEM((n, slab, columns), BF16),
            pltpu.VMEM((3, rows, inner), F32),
            pltpu.VMEM((3, heads, rows, head_size), BF16),
            pltpu.VMEM((n, half, head_size), BF16),
            pltpu.VMEM((2, n, rows, head_size), BF16),
            pltpu.VMEM((n, half, head_size), F32),
            pltpu.VMEM((n, half, head_size), F32),
            pltpu.VMEM((n, half + slab, head_size), BF16),
            pltpu.VMEM((parts, heads, 2 * (half + slab), head_size), BF16),
            dma((11,)), dma((parts,)), dma((parts,)), dma((n,)), dma((n,)), dma((n,)), dma((n,)),
            dma((parts,)), dma((parts,)),
            dma((heads, 2)), dma((n,)), dma((2, heads)), dma((2, n)), dma((2, n)), dma((n,)),
            dma((parts, heads, 2)), dma((parts, heads)), dma((parts // 2 - 1, parts, heads)),
        ],
        compiler_params=pltpu.CompilerParams(
            collective_id=0, has_side_effects=True, vmem_limit_bytes=60 * 1024 * 1024
        ),
    )(
        head_slot, levels, q_gain.reshape(1, -1), k_gain.reshape(1, -1), fresh_noise, latents,
        jnp.transpose(ada_weight, (1, 0, 2)),
        jnp.transpose(qkv_weight, (1, 0, 2)).reshape(3, parts, columns, inner), out_weight,
    )
    updated = pltpu.with_memory_space_constraint(updated, pltpu.VMEM)
    window, clean = pl.pallas_call(
        finish_kernel,
        out_shape=(
            jax.ShapeDtypeStruct((rows, columns), BF16),
            jax.ShapeDtypeStruct((slab, columns), BF16),
        ),
        in_specs=[vmem],
        out_specs=(vmem, vmem),
    )(updated)
    if clean_rows < slab:
        start = (lax.axis_index("seq") * clean_rows) % slab
        clean = lax.dynamic_slice_in_dim(clean, start, clean_rows, 0)
    return window, clean


def solution(mesh):
    return jax.shard_map(
        local,
        mesh=mesh,
        in_specs=(
            P("seq", None),
            P("seq"),
            P(),
            P(None, "tensor"),
            P(None, None, "tensor"),
            P(None, None, "tensor"),
            P(),
            P(),
            P("tensor", None),
        ),
        out_specs=(P("seq", "tensor"), P("seq", "tensor")),
        check_vma=False,
    )
```

```python
import functools
import math

import jax
import jax.numpy as jnp
from jax import lax
from jax.experimental import pallas as pl
from jax.experimental.pallas import tpu as pltpu
from jax.sharding import PartitionSpec as P

F32 = jnp.float32
BF16 = jnp.bfloat16
EPS = 1e-06


def dot(a, b):
    return jnp.dot(a, b, preferred_element_type=F32)


def dot_t(a, b):
    return lax.dot_general(a, b, (((1,), (1,)), ((), ())), preferred_element_type=F32)


def kernel(
    n, parts, slab, clean_rows,
    head_ref, level_ref, q_gain_hbm, k_gain_hbm, noise_hbm, lat_hbm, ada_hbm, qkv_hbm, out_hbm,
    updated_ref,
    gains, noise, lat, ada, wqkv, wout, normed, mods, gates,
    lat_rows, raw, stage, queries, kv, acc, totals, result, attended,
    load_sem, mod_send, mod_recv, gate_sem, row_sem, w_send, w_recv,
    q_sem, kv_send, kv_recv, relay_send, back_send, direct_recv, cross_recv, sib_recv, pass_send,
):
    me = lax.axis_index("seq")
    part = lax.axis_index("tensor")
    pair = 2
    core = lax.rem(part, pair)
    plane = part // pair
    planes = parts // pair
    sibling = plane * pair + 1 - core
    lane = lax.rem(me, pair)
    spot = me // pair
    line = n // pair
    buddy = me + 1 - pair * lane
    rows, width = lat.shape
    columns = updated_ref.shape[1]
    inner = wout.shape[1]
    head_size = gains.shape[2]
    heads = stage.shape[1]
    half = rows // pair
    piece = half + slab
    owners = heads * pair
    first = (n - owners) // 2
    mine = me - first
    active = (mine >= 0) & (mine < owners)
    own_head = jnp.clip(mine // pair, 0, heads - 1)
    own_core = lax.rem(mine + owners * n, pair)
    local = own_core == core
    others = [
        lax.rem(plane + step, planes) * pair + which
        for step in range(1, planes) for which in range(pair)
    ]

    def remote(src, dst, send, recv, target):
        return pltpu.make_async_remote_copy(
            src_ref=src, dst_ref=dst, send_sem=send, recv_sem=recv,
            device_id=target, device_id_type=pl.DeviceIdType.MESH,
        )

    def landed(ref, sem):
        remote(ref, ref, sem, sem, {"tensor": sibling}).wait_recv()

    def sent(ref, sem):
        remote(ref, ref, sem, sem, {"tensor": sibling}).wait_send()

    def at_core(seq, which):
        return {"seq": seq, "tensor": plane * pair + which}

    loads = [
        pltpu.make_async_copy(ada_hbm.at[0:2], ada.at[0:2], load_sem.at[0]),
        pltpu.make_async_copy(lat_hbm, lat, load_sem.at[1]),
        pltpu.make_async_copy(qkv_hbm.at[0], wqkv.at[0], load_sem.at[2]),
        pltpu.make_async_copy(qkv_hbm.at[1], wqkv.at[1], load_sem.at[3]),
        pltpu.make_async_copy(qkv_hbm.at[2], wqkv.at[2], load_sem.at[4]),
        pltpu.make_async_copy(ada_hbm.at[2], ada.at[2], load_sem.at[5]),
        pltpu.make_async_copy(q_gain_hbm, gains.at[0], load_sem.at[6]),
        pltpu.make_async_copy(k_gain_hbm, gains.at[1], load_sem.at[7]),
        pltpu.make_async_copy(
            out_hbm.at[:, pl.ds(pl.multiple_of(part * columns, 128), columns)],
            wout.at[part], load_sem.at[8],
        ),
        pltpu.make_async_copy(noise_hbm, noise, load_sem.at[9]),
    ]
    barrier = pltpu.get_barrier_semaphore()

    @pl.loop(1, n)
    def _(step):
        for which in range(pair):
            pl.semaphore_signal(
                barrier, inc=1, device_id=at_core(lax.rem(me + step, n), which),
                device_id_type=pl.DeviceIdType.MESH,
            )

    for slot in [sibling] + others:
        pl.semaphore_signal(
            barrier, inc=1, device_id={"tensor": slot}, device_id_type=pl.DeviceIdType.MESH
        )
    for load in loads:
        load.start()

    half_width = ada.shape[1] // 2
    order = lax.broadcasted_iota(jnp.int32, (16, half_width), 1).astype(F32)
    angles = level_ref[0].astype(F32) * jnp.exp(-math.log(10000.0) * order / half_width)
    waves = jnp.concatenate([jnp.cos(angles), jnp.sin(angles)], axis=1)
    emb = (waves * (1.0 / (1.0 + jnp.exp(-waves)))).astype(BF16)
    loads[0].wait()
    for j in range(2):
        mods[part, j : j + 1, :] = dot(emb, ada[j])[0:1]

    pl.semaphore_wait(barrier, pair * n - 1 + parts - pair)


    def mod_copy(target, near):
        return remote(
            mods.at[part], mods.at[part], mod_send.at[0], mod_recv.at[near], {"tensor": target}
        )

    for slot in others:
        mod_copy(slot, 1).start()
    mod_copy(sibling, 0).start()

    third = inner // 3 // 16 * 16
    own_third = pl.ds(pl.multiple_of(inner - (pair - lane) * third, 16), third)
    always = pl.ds(0, inner - pair * third)

    def w_copy(target, span, send, recv):
        at = pl.ds(pl.multiple_of(target * columns, 128), columns)
        return remote(
            out_hbm.at[span, at], wout.at[part, span], w_send.at[send], w_recv.at[recv],
            {"tensor": target},
        )

    for slot in others:
        w_copy(slot, own_third, 0, 0).start()
    for slot in others:
        w_copy(slot, always, 0, 1).start()
    w_copy(sibling, pl.ds(0, inner), 1, 2).start()

    def slab_of(device):
        return pl.multiple_of((device * clean_rows) // slab * slab, slab)

    first_column = pl.multiple_of(part * columns, 128)

    def row_copy(target):
        return remote(
            lat_hbm.at[pl.ds(slab_of(target), slab), pl.ds(first_column, columns)],
            lat_rows.at[me], row_sem.at[0], row_sem.at[1], {"seq": target},
        )

    def gate_copy(target):
        return remote(
            gates.at[me], gates.at[me], gate_sem.at[0], gate_sem.at[1], {"seq": target}
        )

    @pl.loop(1, n)
    def _(step):
        row_copy(lax.rem(me + step, n)).start()

    loads[1].wait()
    own_slab = slab_of(me)
    lat_rows[me] = lat[pl.ds(own_slab, slab), pl.ds(first_column, columns)]

    tile = 16

    @pl.loop(0, rows // tile, unroll=4)
    def _(index):
        at = pl.ds(pl.multiple_of(index * tile, tile), tile)
        states = lat[at, :].astype(F32)
        centered = states - jnp.mean(states, axis=-1, keepdims=True)
        variance = jnp.mean(centered * centered, axis=-1, keepdims=True)
        scaled_rows = centered * lax.rsqrt(variance + EPS)
        for index in range(parts):
            normed[index, at, :] = scaled_rows[:, index * columns : (index + 1) * columns]

    def hidden_of(slot):
        return (normed[slot] * (1.0 + mods[slot, 1:2, :]) + mods[slot, 0:1, :]).astype(BF16)

    own_hidden = hidden_of(part)
    for kind in range(3):
        loads[2 + kind].wait()
        raw[kind] = dot(own_hidden, wqkv[kind, part])
    loads[5].wait()
    gates[me] = dot(emb, ada[2])[0:1]

    @pl.loop(1, n)
    def _(step):
        gate_copy(lax.rem(me + step, n)).start()

    landed(mods.at[0], mod_recv.at[0])
    sib_hidden = hidden_of(sibling)
    for kind in range(3):
        raw[kind] += dot(sib_hidden, wqkv[kind, sibling])

    loads[6].wait()
    loads[7].wait()
    landed(mods.at[0 : parts - pair], mod_recv.at[1])
    rest = [hidden_of(slot) for slot in others]

    def whole(kind):
        total = raw[kind]
        for hidden, slot in zip(rest, others):
            total = total + dot(hidden, wqkv[kind, slot])
        return total

    def scaled(matrix, gain, factor):
        power = jnp.mean(matrix * matrix, axis=-1, keepdims=True)
        return (matrix * lax.rsqrt(power + EPS) * gain * factor).astype(BF16)

    def head_at(index):
        return slice(index * head_size, (index + 1) * head_size)

    def turn(step):
        return jnp.where(me < n // 2, heads - 1 - step, step)

    def owner_of(h):
        return first + pair * h + core

    def q_each(act):
        for step in range(heads):
            h = turn(step)
            for which in range(pair):

                @pl.when((owner_of(h) != me) | (core != which))
                def _():
                    act(remote(
                        stage.at[0, h, pl.ds(which * half, half)], queries.at[me],
                        q_sem.at[0], q_sem.at[1], at_core(owner_of(h), which),
                    ))

    def kv_each(kind, act):
        for step in range(heads):
            h = turn(step)
            owner = owner_of(h)
            which = jnp.where(owner == me, 1 - core, lane)
            relayed = jnp.where(which == lane, 0, 1)
            place = lane * line + lax.rem(spot - owner // pair + line, line)
            act(remote(
                stage.at[1 + kind, h], kv.at[kind, place], kv_send.at[0],
                kv_recv.at[kind, relayed], at_core(owner, which),
            ))

    value = whole(0)
    for h in range(heads):
        stage[0, h] = scaled(value[:, head_at(h)], gains[0], 1.0 / math.sqrt(head_size))
    q_each(lambda copy: copy.start())
    value = whole(1)
    for h in range(heads):
        stage[1, h] = scaled(value[:, head_at(h)], gains[1], 1.0)
    kv_each(0, lambda copy: copy.start())
    value = whole(2)
    for h in range(heads):
        stage[2, h] = value[:, head_at(h)].astype(BF16)
    kv_each(1, lambda copy: copy.start())

    landed(wout.at[0 : parts - pair, 0:third], w_recv.at[0])

    def w_pass(slot):
        held = wout.at[slot, own_third]
        return remote(held, held, w_send.at[2], w_recv.at[3], {"seq": buddy})

    for slot in others:
        w_pass(slot).start()

    oldest = head_ref[0]

    def rank_of(block):
        return lax.rem(block - oldest + n, n)

    def column_landed(kind, relayed, column):
        base = column * line

        @pl.when(local & (column == lane))
        def _():
            landed(kv.at[kind, 0 : line - 1], kv_recv.at[kind, relayed])

        @pl.when(jnp.logical_not(local & (column == lane)))
        def _():
            landed(kv.at[kind, 0:line], kv_recv.at[kind, relayed])

    def relay(kind, skip):
        held = kv.at[kind, pl.ds(core * line + skip, line - skip)]
        return remote(
            held, held, relay_send.at[0], kv_recv.at[kind, 1], {"tensor": sibling}
        )

    def relay_on(kind):
        @pl.when(core == lane)
        def _():
            relay(kind, 1).start()

        @pl.when(core != lane)
        def _():
            relay(kind, 0).start()

    slot_at = plane * pair + own_core
    own_piece = pl.ds(pl.multiple_of(core * piece, 16), piece)

    def back_copy(target):
        return remote(
            result.at[target], attended.at[slot_at, own_head, own_piece],
            back_send.at[0], direct_recv.at[own_head * pair + own_core], at_core(target, core),
        )

    span = min(line, 4)

    def absorb(column, base, count, fresh):
        def some(base, start, fresh):
            at = pl.ds(base, count)
            where = pl.ds(column * line + start, span)
            q = queries[at].reshape(count * half, head_size)
            scores = dot_t(q, kv[0, where].reshape(span * rows, head_size))
            ranks = [
                rank_of(lax.rem(spot + start + index, line) * pair + column)
                for index in range(span)
            ]
            joined = []
            for block in range(count):
                rank = rank_of(base + block)
                each = [
                    jnp.exp(
                        scores[block * half : (block + 1) * half, index * rows : (index + 1) * rows]
                        + jnp.where(ranks[index] <= rank, 0.0, -1e30)
                    )
                    for index in range(span)
                ]
                total = functools.reduce(jnp.add, each)
                totals[base + block] = total if fresh else totals[base + block] + total
                joined.append(jnp.concatenate([w.astype(BF16) for w in each], axis=1))
            product = dot(
                jnp.concatenate(joined, axis=0), kv[1, where].reshape(span * rows, head_size)
            ).reshape(count, half, head_size)
            acc[at] = product if fresh else acc[at] + product

        if line == span:
            some(base, 0, fresh)
        else:
            pl.loop(0, line // span)(lambda index: some(base, index * span, False))


    @pl.when(active)
    def _():
        if line != span:
            acc[...] = jnp.zeros_like(acc)
            totals[...] = jnp.zeros_like(totals)

        @pl.when(local)
        def _():
            queries[me] = stage[0, own_head, pl.ds(pl.multiple_of(core * half, half), half)]
            for kind in range(2):
                kv[kind, lane * line] = stage[1 + kind, own_head]
            landed(queries.at[0 : n - 1], q_sem.at[1])

        @pl.when(jnp.logical_not(local))
        def _():
            landed(queries, q_sem.at[1])

        column_landed(0, 0, core)
        relay_on(0)
        column_landed(1, 0, core)
        relay_on(1)
        blocks = min(n, 8)
        if n == blocks:
            absorb(core, 0, n, True)
        else:
            pl.loop(0, n // blocks)(lambda index: absorb(core, index * blocks, blocks, False))
        column_landed(0, 1, 1 - core)
        column_landed(1, 1, 1 - core)

        place = lax.rem(oldest, pair) * line + lax.rem(oldest // pair - spot + line, line)
        weights = jnp.exp(dot_t(queries[oldest], kv[0, place]))
        lead = dot(weights.astype(BF16), kv[1, place])
        lead = (lead / jnp.sum(weights, axis=-1, keepdims=True)).astype(BF16)

        def slab_fill(block):
            at = lax.rem(slab_of(block), half)
            chosen = lead[0:slab]
            for index in range(1, half // slab):
                chosen = jnp.where(
                    jnp.full((slab, head_size), at, jnp.int32) == index * slab,
                    lead[index * slab : (index + 1) * slab], chosen,
                )
            result[block, half:] = chosen

        batch = min(n // 2, 4)

        def batch_at(step):
            return jnp.where(me < n // 2, n // batch - 1 - step, step) * batch

        def last(step):
            base = batch_at(step)
            absorb(1 - core, base, batch, False)
            for index in range(batch):
                block = base + index
                total = jnp.sum(totals[block], axis=-1, keepdims=True)
                result[block, 0:half] = (acc[block] / total).astype(BF16)
                slab_fill(block)
            for index in range(batch):
                target = base + index

                @pl.when(target != me)
                def _():
                    back_copy(target).start()

        if n == 2 * batch:
            last(0)
            last(1)
        else:
            pl.loop(0, n // batch)(last)
        attended[slot_at, own_head, own_piece] = result[me]

    sent(mods.at[0 : parts - 1], mod_send.at[0])

    @pl.when(active & local)
    def _():
        sent(queries.at[0 : owners - 1], q_sem.at[0])

    @pl.when(jnp.logical_not(active & local))
    def _():
        sent(queries.at[0:owners], q_sem.at[0])

    sent(kv.at[:, 0:heads], kv_send.at[0])
    sent(gates.at[0 : n - 1], gate_sem.at[0])
    landed(gates.at[0 : n - 1], gate_sem.at[1])
    sent(lat_rows.at[0 : n - 1], row_sem.at[0])
    landed(lat_rows.at[0 : n - 1], row_sem.at[1])

    def region(slot, h):
        return attended.at[slot, h, own_piece]

    def to_sibling(slot, h, kind):
        held = region(slot, h)
        return remote(
            held, held, pass_send.at[0], sib_recv.at[kind], {"tensor": sibling}
        )

    def across(slot, h, g, step):
        held = region(slot, h)
        return remote(
            held, held, pass_send.at[1], cross_recv.at[step - 1, g],
            {"tensor": lax.rem(plane + step, planes) * pair + core},
        )

    def ordered(step):
        g = jnp.where(me < n // 2, step, owners - 1 - step)
        return g, plane * pair + lax.rem(g, pair), g // pair

    for step in range(owners):
        g, slot, h = ordered(step)

        @pl.when(first + g != me)
        def _():
            landed(region(slot, h), direct_recv.at[g])

        for way in range(1, planes):
            across(slot, h, g, way).start()
        to_sibling(slot, h, 0).start()

    def slot_dot(slot):
        joined = jnp.concatenate([attended[slot, h] for h in range(heads)], axis=1)
        return dot(joined, wout[slot])

    for way in range(1, planes):
        for step in range(owners):
            g, slot, h = ordered(step)
            slot = lax.rem(slot + (planes - way) * pair, parts)
            landed(region(slot, h), cross_recv.at[way - 1, g])
            to_sibling(slot, h, 1).start()

    loads[8].wait()
    landed(wout.at[0], w_recv.at[2])
    landed(attended.at[0:pair, :, 0:piece], sib_recv.at[0])
    total = slot_dot(part) + slot_dot(sibling)
    landed(wout.at[0 : parts - pair, always], w_recv.at[1])
    landed(wout.at[0 : parts - pair, 0:third], w_recv.at[3])
    landed(attended.at[0 : parts - pair, :, 0:piece], sib_recv.at[1])
    for slot in others:
        total = total + slot_dot(slot)

    own_rank = rank_of(me)
    own_states = lat[:, pl.ds(first_column, columns)].astype(F32)
    mixed = jnp.concatenate([total[0:half], total[piece : piece + half]], axis=0)
    updated = (own_states + gates[me] * mixed).astype(BF16)
    leaving = jnp.full((rows, columns), own_rank, jnp.int32) == 0
    loads[9].wait()
    updated_ref[0:rows, :] = jnp.where(leaving, noise[...], updated)
    upper = jnp.full((slab, columns), own_slab, jnp.int32) >= half
    clean = jnp.where(upper, total[piece + half :], total[half:piece])
    updated_ref[rows:, :] = (
        lat_rows[oldest].astype(F32) + gates[oldest] * clean
    ).astype(BF16)

    sent(wout.at[0 : parts - pair, 0 : inner - third], w_send.at[0])
    sent(wout.at[0], w_send.at[1])
    sent(wout.at[0 : parts - pair, 0:third], w_send.at[2])
    sent(attended.at[:, :, 0:piece], pass_send.at[0])
    sent(attended.at[0 : parts - pair, :, 0:piece], pass_send.at[1])

    @pl.when(active)
    def _():
        sent(result.at[0 : n - 1], back_send.at[0])

        @pl.when(core == lane)
        def _():
            sent(kv.at[:, 0 : line - 1], relay_send.at[0])

        @pl.when(core != lane)
        def _():
            sent(kv.at[:, 0:line], relay_send.at[0])


def finish_kernel(updated_ref, window_ref, clean_ref):
    rows = window_ref.shape[0]
    window_ref[...] = updated_ref[0:rows, :]
    clean_ref[...] = updated_ref[rows:, :]


def local(
    latents, levels, head_slot, fresh_noise, ada_weight, qkv_weight, q_gain, k_gain, out_weight
):
    n = lax.axis_size("seq")
    parts = lax.axis_size("tensor")
    rows, width = latents.shape
    columns = fresh_noise.shape[1]
    inner = out_weight.shape[0]
    clean_rows = rows // n
    slab = max(clean_rows, 16)
    heads = inner // q_gain.shape[0]
    head_size = q_gain.shape[0]
    half = rows // 2
    owners = 2 * heads
    vmem = pl.BlockSpec(memory_space=pltpu.VMEM)
    smem = pl.BlockSpec(memory_space=pltpu.SMEM)
    hbm = pl.BlockSpec(memory_space=pltpu.HBM)
    dma = pltpu.SemaphoreType.DMA
    updated = pl.pallas_call(
        functools.partial(kernel, n, parts, slab, clean_rows),
        out_shape=pltpu.VMEM((rows + slab, columns), BF16),
        in_specs=[
            smem, smem, hbm, hbm, hbm, hbm, hbm, hbm, hbm,
        ],
        out_specs=vmem,
        scratch_shapes=[
            pltpu.VMEM((2, 1, head_size), F32),
            pltpu.VMEM((rows, columns), BF16),
            pltpu.VMEM((rows, width), BF16),
            pltpu.VMEM((3, ada_weight.shape[0], columns), BF16),
            pltpu.VMEM((3, parts, columns, inner), BF16),
            pltpu.VMEM((parts, inner, columns), BF16),
            pltpu.VMEM((parts, rows, columns), F32),
            pltpu.VMEM((parts, 2, columns), F32),
            pltpu.VMEM((n, 1, columns), F32),
            pltpu.VMEM((n, slab, columns), BF16),
            pltpu.VMEM((3, rows, inner), F32),
            pltpu.VMEM((3, heads, rows, head_size), BF16),
            pltpu.VMEM((n, half, head_size), BF16),
            pltpu.VMEM((2, n, rows, head_size), BF16),
            pltpu.VMEM((n, half, head_size), F32),
            pltpu.VMEM((n, half, rows), F32),
            pltpu.VMEM((n, half + slab, head_size), BF16),
            pltpu.VMEM((parts, heads, 2 * (half + slab), head_size), BF16),
            dma((10,)), dma((1,)), dma((2,)), dma((2,)), dma((2,)), dma((3,)), dma((4,)),
            dma((2,)), dma((1,)), dma((2, 2)), dma((1,)), dma((1,)), dma((owners,)),
            dma((parts // 2 - 1, owners)), dma((2,)), dma((2,)),
        ],
        compiler_params=pltpu.CompilerParams(
            collective_id=0, has_side_effects=True, vmem_limit_bytes=60 * 1024 * 1024
        ),
    )(
        head_slot, levels, q_gain.reshape(1, -1), k_gain.reshape(1, -1), fresh_noise, latents,
        jnp.transpose(ada_weight, (1, 0, 2)),
        jnp.transpose(qkv_weight, (1, 0, 2)).reshape(3, parts, columns, inner), out_weight,
    )
    updated = pltpu.with_memory_space_constraint(updated, pltpu.VMEM)
    window, clean = pl.pallas_call(
        finish_kernel,
        out_shape=(
            jax.ShapeDtypeStruct((rows, columns), BF16),
            jax.ShapeDtypeStruct((slab, columns), BF16),
        ),
        in_specs=[vmem],
        out_specs=(vmem, vmem),
    )(updated)
    if clean_rows < slab:
        start = (lax.axis_index("seq") * clean_rows) % slab
        clean = lax.dynamic_slice_in_dim(clean, start, clean_rows, 0)
    return window, clean


def solution(mesh):
    return jax.shard_map(
        local,
        mesh=mesh,
        in_specs=(
            P("seq", None),
            P("seq"),
            P(),
            P(None, "tensor"),
            P(None, None, "tensor"),
            P(None, None, "tensor"),
            P(),
            P(),
            P("tensor", None),
        ),
        out_specs=(P("seq", "tensor"), P("seq", "tensor")),
        check_vma=False,
    )
```

```python
import functools
import math

import jax
import jax.numpy as jnp
from jax import lax
from jax.experimental import pallas as pl
from jax.experimental.pallas import tpu as pltpu
from jax.sharding import PartitionSpec as P

F32 = jnp.float32
BF16 = jnp.bfloat16
EPS = 1e-06


def dot(a, b):
    return jnp.dot(a, b, preferred_element_type=F32)


def dot_t(a, b):
    return lax.dot_general(a, b, (((1,), (1,)), ((), ())), preferred_element_type=F32)


def kernel(
    n, parts, slab, clean_rows,
    head_ref, level_ref, q_gain_hbm, k_gain_hbm, noise_hbm, lat_hbm, ada_hbm, qkv_hbm, out_hbm,
    updated_ref,
    gains, noise, lat, ada, wqkv, wout, normed, mods, gates,
    lat_rows, mixed_rows, clean_rows_ref, raw, stage, queries, kv, acc, totals, result, attended,
    ready, load_sem, mod_send, mod_recv, gate_sem, row_sem, w_send, w_recv,
    q_sem, kv_send, kv_recv, relay_send, back_send, direct_recv, cross_recv, sib_recv, pass_send,
):
    me = lax.axis_index("seq")
    part = lax.axis_index("tensor")
    pair = 2
    core = lax.rem(part, pair)
    plane = part // pair
    planes = parts // pair
    sibling = plane * pair + 1 - core
    lane = lax.rem(me, pair)
    spot = me // pair
    line = n // pair
    buddy = me + 1 - pair * lane
    rows, width = lat.shape
    columns = updated_ref.shape[1]
    inner = wout.shape[1]
    head_size = gains.shape[2]
    heads = stage.shape[1]
    half = rows // pair
    piece = half + slab
    owners = heads * pair
    first = (n - owners) // 2
    mine = me - first
    active = (mine >= 0) & (mine < owners)
    own_head = jnp.clip(mine // pair, 0, heads - 1)
    own_core = lax.rem(mine + owners * n, pair)
    local = own_core == core
    others = [
        lax.rem(plane + step, planes) * pair + lax.rem(core + which, pair)
        for step in range(1, planes) for which in range(pair)
    ]

    def remote(src, dst, send, recv, target):
        return pltpu.make_async_remote_copy(
            src_ref=src, dst_ref=dst, send_sem=send, recv_sem=recv,
            device_id=target, device_id_type=pl.DeviceIdType.MESH,
        )

    def landed(ref, sem):
        remote(ref, ref, sem, sem, {"tensor": sibling}).wait_recv()

    def sent(ref, sem):
        remote(ref, ref, sem, sem, {"tensor": sibling}).wait_send()

    def at_core(seq, which):
        return {"seq": seq, "tensor": plane * pair + which}

    loads = [
        pltpu.make_async_copy(ada_hbm.at[0:2], ada.at[0:2], load_sem.at[0]),
        pltpu.make_async_copy(lat_hbm, lat, load_sem.at[1]),
        pltpu.make_async_copy(qkv_hbm.at[0], wqkv.at[0], load_sem.at[2]),
        pltpu.make_async_copy(qkv_hbm.at[1], wqkv.at[1], load_sem.at[3]),
        pltpu.make_async_copy(qkv_hbm.at[2], wqkv.at[2], load_sem.at[4]),
        pltpu.make_async_copy(ada_hbm.at[2], ada.at[2], load_sem.at[5]),
        pltpu.make_async_copy(q_gain_hbm, gains.at[0], load_sem.at[6]),
        pltpu.make_async_copy(k_gain_hbm, gains.at[1], load_sem.at[7]),
        pltpu.make_async_copy(
            out_hbm.at[:, pl.ds(pl.multiple_of(part * columns, 128), columns)],
            wout.at[part], load_sem.at[8],
        ),
        pltpu.make_async_copy(noise_hbm, noise, load_sem.at[9]),
    ]
    barrier = pltpu.get_barrier_semaphore()

    @pl.loop(1, n)
    def _(step):
        pl.semaphore_signal(
            barrier, inc=1, device_id=at_core(lax.rem(me + step, n), pair - 1),
            device_id_type=pl.DeviceIdType.MESH,
        )

    for step in range(planes):
        slot = lax.rem(plane + step, planes) * pair

        @pl.when(slot != part)
        def _():
            pl.semaphore_signal(
                barrier, inc=1, device_id={"tensor": slot}, device_id_type=pl.DeviceIdType.MESH
            )

    for load in loads:
        load.start()

    half_width = ada.shape[1] // 2
    order = lax.broadcasted_iota(jnp.int32, (16, half_width), 1).astype(F32)
    angles = level_ref[0].astype(F32) * jnp.exp(-math.log(10000.0) * order / half_width)
    waves = jnp.concatenate([jnp.cos(angles), jnp.sin(angles)], axis=1)
    emb = (waves * (1.0 / (1.0 + jnp.exp(-waves)))).astype(BF16)
    loads[0].wait()
    for j in range(2):
        mods[part, j : j + 1, :] = dot(emb, ada[j])[0:1]

    def tell_sibling():
        pl.semaphore_signal(
            ready, inc=1, device_id={"tensor": sibling}, device_id_type=pl.DeviceIdType.MESH
        )

    @pl.when(core == 0)
    def _():
        pl.semaphore_wait(barrier, parts - 1)
        tell_sibling()

    @pl.when(core != 0)
    def _():
        pl.semaphore_wait(ready, 1)

    def meet():
        @pl.when(core != 0)
        def _():
            pl.semaphore_wait(barrier, pair * (n - 1))
            tell_sibling()

        @pl.when(core == 0)
        def _():
            pl.semaphore_wait(ready, 1)


    def mod_copy(target, near):
        return remote(
            mods.at[part], mods.at[part], mod_send.at[0], mod_recv.at[near], {"tensor": target}
        )

    for slot in others:
        mod_copy(slot, 1).start()
    mod_copy(sibling, 0).start()

    third = inner // 3 // 16 * 16
    own_third = pl.ds(pl.multiple_of(inner - (pair - lane) * third, 16), third)
    always = pl.ds(0, inner - pair * third)

    def w_copy(target, span, send, recv):
        at = pl.ds(pl.multiple_of(target * columns, 128), columns)
        return remote(
            out_hbm.at[span, at], wout.at[part, span], w_send.at[send], w_recv.at[recv],
            {"tensor": target},
        )

    for index, slot in enumerate(others):
        w_copy(slot, own_third, 0, 4 + index).start()
    for slot in others:
        w_copy(slot, always, 0, 1).start()
    w_copy(sibling, pl.ds(0, inner), 1, 2).start()

    def slab_of(device):
        return pl.multiple_of((device * clean_rows) // slab * slab, slab)

    first_column = pl.multiple_of(part * columns, 128)

    def swap_copy(step):
        return remote(
            lat_hbm.at[pl.ds(slab_of(step * pair + 1 - lane), slab), pl.ds(first_column, columns)],
            lat_rows.at[step], row_sem.at[0], row_sem.at[1], {"seq": buddy},
        )

    def gate_copy(target):
        return remote(
            gates.at[me], gates.at[me], gate_sem.at[0], gate_sem.at[1], {"seq": target}
        )

    loads[1].wait()
    own_slab = slab_of(me)

    tile = 16

    @pl.loop(0, rows // tile, unroll=4)
    def _(index):
        at = pl.ds(pl.multiple_of(index * tile, tile), tile)
        states = lat[at, :].astype(F32)
        centered = states - jnp.mean(states, axis=-1, keepdims=True)
        variance = jnp.mean(centered * centered, axis=-1, keepdims=True)
        scaled_rows = centered * lax.rsqrt(variance + EPS)
        for index in range(parts):
            normed[index, at, :] = scaled_rows[:, index * columns : (index + 1) * columns]

    def hidden_of(slot):
        return (normed[slot] * (1.0 + mods[slot, 1:2, :]) + mods[slot, 0:1, :]).astype(BF16)

    own_hidden = hidden_of(part)
    for kind in range(3):
        loads[2 + kind].wait()
        raw[kind] = dot(own_hidden, wqkv[kind, part])
    landed(mods.at[0], mod_recv.at[0])
    sib_hidden = hidden_of(sibling)
    for kind in range(3):
        raw[kind] += dot(sib_hidden, wqkv[kind, sibling])

    loads[6].wait()
    loads[7].wait()
    landed(mods.at[0 : parts - pair], mod_recv.at[1])
    rest = [hidden_of(slot) for slot in others]

    def whole(kind):
        total = raw[kind]
        for hidden, slot in zip(rest, others):
            total = total + dot(hidden, wqkv[kind, slot])
        return total

    def scaled(matrix, gain, factor):
        power = jnp.mean(matrix * matrix, axis=-1, keepdims=True)
        return (matrix * lax.rsqrt(power + EPS) * gain * factor).astype(BF16)

    def head_at(index):
        return slice(index * head_size, (index + 1) * head_size)

    def turn(step):
        return jnp.where(me < n // 2, heads - 1 - step, step)

    def owner_of(h):
        return first + pair * h + core

    def q_each(act):
        for step in range(heads):
            h = turn(step)
            for which in range(pair):

                @pl.when((owner_of(h) != me) | (core != which))
                def _():
                    act(remote(
                        stage.at[0, h, pl.ds(which * half, half)], queries.at[me],
                        q_sem.at[0], q_sem.at[1], at_core(owner_of(h), which),
                    ))

    def kv_each(kind, act):
        for step in range(heads):
            h = turn(step)
            owner = owner_of(h)
            which = jnp.where(owner == me, 1 - core, lane)
            relayed = jnp.where(which == lane, 0, 1)
            place = lane * line + lax.rem(spot - owner // pair + line, line)
            act(remote(
                stage.at[1 + kind, h], kv.at[kind, place], kv_send.at[0],
                kv_recv.at[kind, relayed], at_core(owner, which),
            ))

    value = whole(0)
    for h in range(heads):
        stage[0, h] = scaled(value[:, head_at(h)], gains[0], 1.0 / math.sqrt(head_size))
    meet()
    q_each(lambda copy: copy.start())
    value = whole(1)
    for h in range(heads):
        stage[1, h] = scaled(value[:, head_at(h)], gains[1], 1.0)
    kv_each(0, lambda copy: copy.start())
    value = whole(2)
    for h in range(heads):
        stage[2, h] = value[:, head_at(h)].astype(BF16)
    kv_each(1, lambda copy: copy.start())

    @pl.loop(0, line)
    def _(step):
        swap_copy(step).start()

    oldest = head_ref[0]
    for index, slot in enumerate(others):
        held = wout.at[slot, own_third]
        landed(held, w_recv.at[4 + index])
        remote(held, held, w_send.at[2], w_recv.at[3], {"seq": buddy}).start()

    def rank_of(block):
        return lax.rem(block - oldest + n, n)

    def column_landed(kind, relayed, column):
        base = column * line

        @pl.when(local & (column == lane))
        def _():
            landed(kv.at[kind, 0 : line - 1], kv_recv.at[kind, relayed])

        @pl.when(jnp.logical_not(local & (column == lane)))
        def _():
            landed(kv.at[kind, 0:line], kv_recv.at[kind, relayed])

    def relay(kind, skip):
        held = kv.at[kind, pl.ds(core * line + skip, line - skip)]
        return remote(
            held, held, relay_send.at[0], kv_recv.at[kind, 1], {"tensor": sibling}
        )

    def relay_on(kind):
        @pl.when(core == lane)
        def _():
            relay(kind, 1).start()

        @pl.when(core != lane)
        def _():
            relay(kind, 0).start()

    slot_at = plane * pair + own_core
    own_piece = pl.ds(pl.multiple_of(core * piece, 16), piece)

    def back_copy(target):
        return remote(
            result.at[target], attended.at[slot_at, own_head, own_piece],
            back_send.at[0], direct_recv.at[own_head * pair + own_core], at_core(target, core),
        )

    span = min(line, 4)

    def absorb(column, base, count, fresh):
        def some(base, start, fresh):
            at = pl.ds(base, count)
            where = pl.ds(column * line + start, span)
            q = queries[at].reshape(count * half, head_size)
            scores = dot_t(q, kv[0, where].reshape(span * rows, head_size))
            ranks = [
                rank_of(lax.rem(spot + start + index, line) * pair + column)
                for index in range(span)
            ]
            joined = []
            for block in range(count):
                rank = rank_of(base + block)
                each = [
                    jnp.exp(
                        scores[block * half : (block + 1) * half, index * rows : (index + 1) * rows]
                        + jnp.where(ranks[index] <= rank, 0.0, -1e30)
                    )
                    for index in range(span)
                ]
                total = functools.reduce(jnp.add, each)
                totals[base + block] = total if fresh else totals[base + block] + total
                joined.append(jnp.concatenate([w.astype(BF16) for w in each], axis=1))
            product = dot(
                jnp.concatenate(joined, axis=0), kv[1, where].reshape(span * rows, head_size)
            ).reshape(count, half, head_size)
            acc[at] = product if fresh else acc[at] + product

        if line == span:
            some(base, 0, fresh)
        else:
            pl.loop(0, line // span)(lambda index: some(base, index * span, False))


    @pl.when(active)
    def _():
        if line != span:
            acc[...] = jnp.zeros_like(acc)
            totals[...] = jnp.zeros_like(totals)

        @pl.when(local)
        def _():
            queries[me] = stage[0, own_head, pl.ds(pl.multiple_of(core * half, half), half)]
            for kind in range(2):
                kv[kind, lane * line] = stage[1 + kind, own_head]
            landed(queries.at[0 : n - 1], q_sem.at[1])

        @pl.when(jnp.logical_not(local))
        def _():
            landed(queries, q_sem.at[1])

        column_landed(0, 0, core)
        relay_on(0)
        column_landed(1, 0, core)
        relay_on(1)
        blocks = min(n, 8)
        if n == blocks:
            absorb(core, 0, n, True)
        else:
            pl.loop(0, n // blocks)(lambda index: absorb(core, index * blocks, blocks, False))
        column_landed(0, 1, 1 - core)
        column_landed(1, 1, 1 - core)

        place = lax.rem(oldest, pair) * line + lax.rem(oldest // pair - spot + line, line)
        weights = jnp.exp(dot_t(queries[oldest], kv[0, place]))
        lead = dot(weights.astype(BF16), kv[1, place])
        lead = (lead / jnp.sum(weights, axis=-1, keepdims=True)).astype(BF16)

        def slab_fill(block):
            at = lax.rem(slab_of(block), half)
            chosen = lead[0:slab]
            for index in range(1, half // slab):
                chosen = jnp.where(
                    jnp.full((slab, head_size), at, jnp.int32) == index * slab,
                    lead[index * slab : (index + 1) * slab], chosen,
                )
            result[block, half:] = chosen

        batch = min(n // 2, 4)

        def batch_at(step):
            return jnp.where(me < n // 2, n // batch - 1 - step, step) * batch

        def last(step):
            base = batch_at(step)
            absorb(1 - core, base, batch, False)
            for index in range(batch):
                block = base + index
                total = jnp.sum(totals[block], axis=-1, keepdims=True)
                result[block, 0:half] = (acc[block] / total).astype(BF16)
                slab_fill(block)
            for index in range(batch):
                target = base + index

                @pl.when(target != me)
                def _():
                    back_copy(target).start()

        if n == 2 * batch:
            last(0)
            last(1)
        else:
            pl.loop(0, n // batch)(last)
        attended[slot_at, own_head, own_piece] = result[me]

    landed(lat_rows, row_sem.at[1])
    swapped = jnp.full((slab, columns), buddy, jnp.int32) == oldest
    for step in range(line):
        target = step * pair + lane
        kept = lat[pl.ds(slab_of(target), slab), pl.ds(first_column, columns)]
        mixed_rows[step] = jnp.where(swapped, lat_rows[step], kept)
    clean_rows_ref[spot] = mixed_rows[spot]

    def row_copy(target_spot):
        return remote(
            mixed_rows.at[target_spot], clean_rows_ref.at[spot], row_sem.at[2], row_sem.at[3],
            {"seq": target_spot * pair + lane},
        )

    @pl.loop(1, line)
    def _(step):
        row_copy(lax.rem(spot + step, line)).start()

    loads[5].wait()
    gates[me] = dot(emb, ada[2])[0:1]

    @pl.loop(1, n)
    def _(step):
        gate_copy(lax.rem(me + step, n)).start()

    def region(slot, h):
        return attended.at[slot, h, own_piece]

    def to_sibling(slot, h, kind):
        held = region(slot, h)
        return remote(
            held, held, pass_send.at[0], sib_recv.at[kind], {"tensor": sibling}
        )

    def across(slot, h, g, step):
        held = region(slot, h)
        return remote(
            held, held, pass_send.at[1], cross_recv.at[step - 1, g],
            {"tensor": lax.rem(plane + step, planes) * pair + core},
        )

    def ordered(step):
        g = jnp.where(me < n // 2, owners - 1 - step, step)
        return g, plane * pair + lax.rem(g, pair), g // pair

    for step in range(owners):
        g, slot, h = ordered(step)

        @pl.when(first + g != me)
        def _():
            landed(region(slot, h), direct_recv.at[g])

        for way in range(1, planes):
            across(slot, h, g, way).start()
        to_sibling(slot, h, 0).start()

    def slot_dot(slot):
        joined = jnp.concatenate([attended[slot, h] for h in range(heads)], axis=1)
        return dot(joined, wout[slot])

    for way in range(1, planes):
        for step in range(owners):
            g, slot, h = ordered(step)
            slot = lax.rem(slot + (planes - way) * pair, parts)
            landed(region(slot, h), cross_recv.at[way - 1, g])
            to_sibling(slot, h, 1).start()

    loads[8].wait()
    landed(wout.at[0], w_recv.at[2])
    landed(attended.at[0:pair, :, 0:piece], sib_recv.at[0])
    total = slot_dot(part) + slot_dot(sibling)
    landed(wout.at[0 : parts - pair, always], w_recv.at[1])
    landed(wout.at[0 : parts - pair, 0:third], w_recv.at[3])
    landed(attended.at[0 : parts - pair, :, 0:piece], sib_recv.at[1])
    for slot in others:
        total = total + slot_dot(slot)

    landed(gates.at[0 : n - 1], gate_sem.at[1])
    landed(lat_rows.at[0 : line - 1], row_sem.at[3])
    loads[9].wait()
    own_rank = rank_of(me)
    own_states = lat[:, pl.ds(first_column, columns)].astype(F32)
    mixed = jnp.concatenate([total[0:half], total[piece : piece + half]], axis=0)
    updated = (own_states + gates[me] * mixed).astype(BF16)
    leaving = jnp.full((rows, columns), own_rank, jnp.int32) == 0
    updated_ref[0:rows, :] = jnp.where(leaving, noise[...], updated)
    upper = jnp.full((slab, columns), own_slab, jnp.int32) >= half
    clean = jnp.where(upper, total[piece + half :], total[half:piece])
    updated_ref[rows:, :] = (
        clean_rows_ref[oldest // pair].astype(F32) + gates[oldest] * clean
    ).astype(BF16)

    sent(mods.at[0 : parts - 1], mod_send.at[0])

    @pl.when(active & local)
    def _():
        sent(queries.at[0 : owners - 1], q_sem.at[0])

    @pl.when(jnp.logical_not(active & local))
    def _():
        sent(queries.at[0:owners], q_sem.at[0])

    sent(kv.at[:, 0:heads], kv_send.at[0])
    sent(gates.at[0 : n - 1], gate_sem.at[0])
    sent(lat_rows, row_sem.at[0])
    sent(lat_rows.at[0 : line - 1], row_sem.at[2])
    sent(wout.at[0 : parts - pair, 0 : inner - third], w_send.at[0])
    sent(wout.at[0], w_send.at[1])
    sent(wout.at[0 : parts - pair, 0:third], w_send.at[2])
    sent(attended.at[:, :, 0:piece], pass_send.at[0])
    sent(attended.at[0 : parts - pair, :, 0:piece], pass_send.at[1])

    @pl.when(active)
    def _():
        sent(result.at[0 : n - 1], back_send.at[0])

        @pl.when(core == lane)
        def _():
            sent(kv.at[:, 0 : line - 1], relay_send.at[0])

        @pl.when(core != lane)
        def _():
            sent(kv.at[:, 0:line], relay_send.at[0])


def finish_kernel(updated_ref, window_ref, clean_ref):
    rows = window_ref.shape[0]
    window_ref[...] = updated_ref[0:rows, :]
    clean_ref[...] = updated_ref[rows:, :]


def local(
    latents, levels, head_slot, fresh_noise, ada_weight, qkv_weight, q_gain, k_gain, out_weight
):
    n = lax.axis_size("seq")
    parts = lax.axis_size("tensor")
    rows, width = latents.shape
    columns = fresh_noise.shape[1]
    inner = out_weight.shape[0]
    clean_rows = rows // n
    slab = max(clean_rows, 16)
    heads = inner // q_gain.shape[0]
    head_size = q_gain.shape[0]
    half = rows // 2
    owners = 2 * heads
    vmem = pl.BlockSpec(memory_space=pltpu.VMEM)
    smem = pl.BlockSpec(memory_space=pltpu.SMEM)
    hbm = pl.BlockSpec(memory_space=pltpu.HBM)
    dma = pltpu.SemaphoreType.DMA
    updated = pl.pallas_call(
        functools.partial(kernel, n, parts, slab, clean_rows),
        out_shape=pltpu.VMEM((rows + slab, columns), BF16),
        in_specs=[
            smem, smem, hbm, hbm, hbm, hbm, hbm, hbm, hbm,
        ],
        out_specs=vmem,
        scratch_shapes=[
            pltpu.VMEM((2, 1, head_size), F32),
            pltpu.VMEM((rows, columns), BF16),
            pltpu.VMEM((rows, width), BF16),
            pltpu.VMEM((3, ada_weight.shape[0], columns), BF16),
            pltpu.VMEM((3, parts, columns, inner), BF16),
            pltpu.VMEM((parts, inner, columns), BF16),
            pltpu.VMEM((parts, rows, columns), F32),
            pltpu.VMEM((parts, 2, columns), F32),
            pltpu.VMEM((n, 1, columns), F32),
            pltpu.VMEM((n // 2, slab, columns), BF16),
            pltpu.VMEM((n // 2, slab, columns), BF16),
            pltpu.VMEM((n // 2, slab, columns), BF16),
            pltpu.VMEM((3, rows, inner), F32),
            pltpu.VMEM((3, heads, rows, head_size), BF16),
            pltpu.VMEM((n, half, head_size), BF16),
            pltpu.VMEM((2, n, rows, head_size), BF16),
            pltpu.VMEM((n, half, head_size), F32),
            pltpu.VMEM((n, half, rows), F32),
            pltpu.VMEM((n, half + slab, head_size), BF16),
            pltpu.VMEM((parts, heads, 2 * (half + slab), head_size), BF16),
            pltpu.SemaphoreType.REGULAR, dma((10,)), dma((1,)), dma((2,)), dma((2,)), dma((4,)), dma((3,)), dma((4 + parts - 2,)),
            dma((2,)), dma((1,)), dma((2, 2)), dma((1,)), dma((1,)), dma((owners,)),
            dma((parts // 2 - 1, owners)), dma((2,)), dma((2,)),
        ],
        compiler_params=pltpu.CompilerParams(
            collective_id=0, has_side_effects=True, vmem_limit_bytes=60 * 1024 * 1024
        ),
    )(
        head_slot, levels, q_gain.reshape(1, -1), k_gain.reshape(1, -1), fresh_noise, latents,
        jnp.transpose(ada_weight, (1, 0, 2)),
        jnp.transpose(qkv_weight, (1, 0, 2)).reshape(3, parts, columns, inner), out_weight,
    )
    updated = pltpu.with_memory_space_constraint(updated, pltpu.VMEM)
    window, clean = pl.pallas_call(
        finish_kernel,
        out_shape=(
            jax.ShapeDtypeStruct((rows, columns), BF16),
            jax.ShapeDtypeStruct((slab, columns), BF16),
        ),
        in_specs=[vmem],
        out_specs=(vmem, vmem),
    )(updated)
    if clean_rows < slab:
        start = (lax.axis_index("seq") * clean_rows) % slab
        clean = lax.dynamic_slice_in_dim(clean, start, clean_rows, 0)
    return window, clean


def solution(mesh):
    return jax.shard_map(
        local,
        mesh=mesh,
        in_specs=(
            P("seq", None),
            P("seq"),
            P(),
            P(None, "tensor"),
            P(None, None, "tensor"),
            P(None, None, "tensor"),
            P(),
            P(),
            P("tensor", None),
        ),
        out_specs=(P("seq", "tensor"), P("seq", "tensor")),
        check_vma=False,
    )
```

```python
import functools
import math

import jax
import jax.numpy as jnp
from jax import lax
from jax.experimental import pallas as pl
from jax.experimental.pallas import tpu as pltpu
from jax.sharding import PartitionSpec as P

F32 = jnp.float32
BF16 = jnp.bfloat16
EPS = 1e-06


def dot(a, b):
    return jnp.dot(a, b, preferred_element_type=F32)


def dot_t(a, b):
    return lax.dot_general(a, b, (((1,), (1,)), ((), ())), preferred_element_type=F32)


def kernel(
    n, parts, slab, clean_rows,
    head_ref, level_ref, q_gain_hbm, k_gain_hbm, noise_hbm, lat_hbm, ada_hbm, qkv_hbm, out_hbm,
    updated_ref,
    gains, noise, lat, ada, wqkv, wout, normed, mods, gates,
    lat_rows, mixed_rows, clean_rows_ref, raw, stage, queries, keys, values, acc, totals, seen, result, attended, partial,
    ready, load_sem, mod_send, mod_recv, gate_sem, row_sem, w_send, w_recv,
    q_sem, kv_send, kv_recv, relay_send, back_send, direct_recv, cross_recv, sib_recv, pass_send,
):
    kv = (keys, values)
    me = lax.axis_index("seq")
    part = lax.axis_index("tensor")
    pair = 2
    core = lax.rem(part, pair)
    plane = part // pair
    planes = parts // pair
    sibling = plane * pair + 1 - core
    lane = lax.rem(me, pair)
    spot = me // pair
    line = n // pair
    buddy = me + 1 - pair * lane
    rows, width = lat.shape
    columns = updated_ref.shape[1]
    inner = wout.shape[1]
    head_size = gains.shape[2]
    heads = stage.shape[1]
    half = rows // pair
    piece = half + slab
    owners = heads * pair
    first = (n - owners) // 2
    mine = me - first
    active = (mine >= 0) & (mine < owners)
    own_head = jnp.clip(mine // pair, 0, heads - 1)
    own_core = lax.rem(mine + owners * n, pair)
    local = own_core == core
    others = [
        lax.rem(plane + step, planes) * pair + lax.rem(core + which, pair)
        for step in range(1, planes) for which in range(pair)
    ]

    def remote(src, dst, send, recv, target):
        return pltpu.make_async_remote_copy(
            src_ref=src, dst_ref=dst, send_sem=send, recv_sem=recv,
            device_id=target, device_id_type=pl.DeviceIdType.MESH,
        )

    def landed(ref, sem):
        remote(ref, ref, sem, sem, {"tensor": sibling}).wait_recv()

    def sent(ref, sem):
        remote(ref, ref, sem, sem, {"tensor": sibling}).wait_send()

    def at_core(seq, which):
        return {"seq": seq, "tensor": plane * pair + which}

    loads = [
        pltpu.make_async_copy(ada_hbm.at[0:2], ada.at[0:2], load_sem.at[0]),
        pltpu.make_async_copy(lat_hbm, lat, load_sem.at[1]),
        pltpu.make_async_copy(qkv_hbm.at[0], wqkv.at[0], load_sem.at[2]),
        pltpu.make_async_copy(qkv_hbm.at[1], wqkv.at[1], load_sem.at[3]),
        pltpu.make_async_copy(qkv_hbm.at[2], wqkv.at[2], load_sem.at[4]),
        pltpu.make_async_copy(ada_hbm.at[2], ada.at[2], load_sem.at[5]),
        pltpu.make_async_copy(q_gain_hbm, gains.at[0], load_sem.at[6]),
        pltpu.make_async_copy(k_gain_hbm, gains.at[1], load_sem.at[7]),
        pltpu.make_async_copy(
            out_hbm.at[:, pl.ds(pl.multiple_of(part * columns, 128), columns)],
            wout.at[part], load_sem.at[8],
        ),
        pltpu.make_async_copy(noise_hbm, noise, load_sem.at[9]),
    ]
    barrier = pltpu.get_barrier_semaphore()

    loads[0].start()
    for step in range(planes):
        slot = lax.rem(plane + step, planes) * pair

        @pl.when(slot != part)
        def _():
            pl.semaphore_signal(
                barrier, inc=1, device_id={"tensor": slot}, device_id_type=pl.DeviceIdType.MESH
            )

    for load in loads[1:5]:
        load.start()

    @pl.loop(1, n)
    def _(step):
        pl.semaphore_signal(
            barrier, inc=1, device_id=at_core(lax.rem(me + step, n), pair - 1),
            device_id_type=pl.DeviceIdType.MESH,
        )


    half_width = ada.shape[1] // 2
    order = lax.broadcasted_iota(jnp.int32, (16, half_width), 1).astype(F32)
    angles = level_ref[0].astype(F32) * jnp.exp(-math.log(10000.0) * order / half_width)
    waves = jnp.concatenate([jnp.cos(angles), jnp.sin(angles)], axis=1)
    emb = (waves * (1.0 / (1.0 + jnp.exp(-waves)))).astype(BF16)
    def tell_sibling():
        pl.semaphore_signal(
            ready, inc=1, device_id={"tensor": sibling}, device_id_type=pl.DeviceIdType.MESH
        )

    @pl.when(core == 0)
    def _():
        pl.semaphore_wait(barrier, parts - 1)
        tell_sibling()

    @pl.when(core != 0)
    def _():
        pl.semaphore_wait(ready, 1)

    loads[0].wait()
    for j in range(2):
        mods[part, j : j + 1, :] = dot(emb, ada[j])[0:1]

    def meet():
        @pl.when(core != 0)
        def _():
            pl.semaphore_wait(barrier, pair * (n - 1))
            tell_sibling()

        @pl.when(core == 0)
        def _():
            pl.semaphore_wait(ready, 1)


    def mod_copy(target, near):
        return remote(
            mods.at[part], mods.at[part], mod_send.at[0], mod_recv.at[near], {"tensor": target}
        )

    for slot in others:
        mod_copy(slot, 1).start()
    mod_copy(sibling, 0).start()

    third = inner // 3 // 16 * 16
    own_third = pl.ds(pl.multiple_of(inner - (pair - lane) * third, 16), third)
    always = pl.ds(0, inner - pair * third)

    def w_copy(target, span, send, recv):
        at = pl.ds(pl.multiple_of(target * columns, 128), columns)
        return remote(
            out_hbm.at[span, at], wout.at[part, span], w_send.at[send], w_recv.at[recv],
            {"tensor": target},
        )

    for index, slot in enumerate(others):
        w_copy(slot, own_third, 0, 4 + index).start()
    for slot in others:
        w_copy(slot, always, 0, 1).start()

    def slab_of(device):
        return pl.multiple_of((device * clean_rows) // slab * slab, slab)

    first_column = pl.multiple_of(part * columns, 128)

    def swap_copy(step):
        return remote(
            lat_hbm.at[pl.ds(slab_of(step * pair + 1 - lane), slab), pl.ds(first_column, columns)],
            lat_rows.at[step], row_sem.at[0], row_sem.at[1], {"seq": buddy},
        )

    def gate_copy(target):
        return remote(
            gates.at[me], gates.at[me], gate_sem.at[0], gate_sem.at[1], {"seq": target}
        )

    loads[1].wait()
    own_slab = slab_of(me)

    tile = 16

    @pl.loop(0, rows // tile, unroll=4)
    def _(index):
        at = pl.ds(pl.multiple_of(index * tile, tile), tile)
        states = lat[at, :].astype(F32)
        centered = states - jnp.mean(states, axis=-1, keepdims=True)
        variance = jnp.mean(centered * centered, axis=-1, keepdims=True)
        scaled_rows = centered * lax.rsqrt(variance + EPS)
        for index in range(parts):
            normed[index, at, :] = scaled_rows[:, index * columns : (index + 1) * columns]

    def hidden_of(slot):
        return (normed[slot] * (1.0 + mods[slot, 1:2, :]) + mods[slot, 0:1, :]).astype(BF16)

    own_hidden = hidden_of(part)
    for kind in range(3):
        loads[2 + kind].wait()
        raw[kind] = dot(own_hidden, wqkv[kind, part])
    for load in loads[5:]:
        load.start()
    landed(mods.at[0], mod_recv.at[0])
    sib_hidden = hidden_of(sibling)
    for kind in range(3):
        raw[kind] += dot(sib_hidden, wqkv[kind, sibling])

    loads[6].wait()
    loads[7].wait()
    landed(mods.at[0 : parts - pair], mod_recv.at[1])
    rest = [hidden_of(slot) for slot in others]

    def whole(kind):
        total = raw[kind]
        for hidden, slot in zip(rest, others):
            total = total + dot(hidden, wqkv[kind, slot])
        return total

    def scaled(matrix, gain, factor):
        power = jnp.mean(matrix * matrix, axis=-1, keepdims=True)
        return (matrix * lax.rsqrt(power + EPS) * gain * factor).astype(BF16)

    def head_at(index):
        return slice(index * head_size, (index + 1) * head_size)

    def turn(step):
        return jnp.where(me < n // 2, heads - 1 - step, step)

    def owner_of(h):
        return first + pair * h + core

    def send(kind, step):
        h = turn(step)
        owner = owner_of(h)
        if kind == 0:
            for which in range(pair):

                @pl.when((owner != me) | (core != which))
                def _():
                    remote(
                        stage.at[0, h, pl.ds(which * half, half)], queries.at[me],
                        q_sem.at[0], q_sem.at[1], at_core(owner, which),
                    ).start()
        else:
            which = jnp.where(owner == me, 1 - core, lane)
            relayed = jnp.where(which == lane, 0, 1)
            place = lane * line + lax.rem(spot - owner // pair + line, line)
            remote(
                stage.at[kind, h], kv[kind - 1].at[place], kv_send.at[0],
                kv_recv.at[jnp.where(relayed == 1, kind - 1, 2 if kind == 1 else 3 + place - lane * line)],
                at_core(owner, which),
            ).start()

    turns = [(kind, step) for step in range(heads) for kind in range(3)]

    def send_ready(kind):
        now = [t for t in turns if t[0] <= kind]
        for t in now:
            turns.remove(t)
            send(*t)

    value = whole(0)
    for h in range(heads):
        stage[0, h] = scaled(value[:, head_at(h)], gains[0], 1.0 / math.sqrt(head_size))
    meet()
    send_ready(0)
    value = whole(1)
    for h in range(heads):
        stage[1, h] = scaled(value[:, head_at(h)], gains[1], 1.0)
    send_ready(1)
    value = whole(2)
    for h in range(heads):
        stage[2, h] = value[:, head_at(h)].astype(BF16)
    send_ready(2)

    w_copy(sibling, pl.ds(0, inner), 1, 2).start()

    @pl.loop(0, line)
    def _(step):
        swap_copy(step).start()

    oldest = head_ref[0]
    loads[5].wait()
    gates[me] = dot(emb, ada[2])[0:1]
    for index, slot in enumerate(others):
        held = wout.at[slot, own_third]
        landed(held, w_recv.at[4 + index])
        remote(held, held, w_send.at[2], w_recv.at[3], {"seq": buddy}).start()

    def rank_of(block):
        return lax.rem(block - oldest + n, n)

    def column_landed(kind, sem, column):
        @pl.when(local & (column == lane))
        def _():
            landed(kv[kind].at[0 : line - 1], kv_recv.at[sem])

        @pl.when(jnp.logical_not(local & (column == lane)))
        def _():
            landed(kv[kind].at[0:line], kv_recv.at[sem])

    def relay(kind, skip):
        held = kv[kind].at[pl.ds(core * line + skip, line - skip)]
        return remote(held, held, relay_send.at[0], kv_recv.at[kind], {"tensor": sibling})

    def values_landed():
        @pl.loop(0, line)
        def _(place):
            held = values.at[core * line + place]
            inside = (place == 0) & (core == lane)

            @pl.when(jnp.logical_not(inside & local))
            def _():
                landed(held, kv_recv.at[3 + place])

            @pl.when(jnp.logical_not(inside))
            def _():
                remote(
                    held, held, relay_send.at[0], kv_recv.at[1], {"tensor": sibling}
                ).start()

    def relay_on(kind):
        @pl.when(core == lane)
        def _():
            relay(kind, 1).start()

        @pl.when(core != lane)
        def _():
            relay(kind, 0).start()

    slot_at = plane * pair + own_core
    own_piece = pl.ds(pl.multiple_of(core * piece, 16), piece)

    def back_copy(target):
        return remote(
            result.at[target], attended.at[slot_at, own_head, own_piece],
            back_send.at[0], direct_recv.at[own_head * pair + own_core], at_core(target, core),
        )

    span = min(line, 4)
    simple = line == span

    def absorb(column, base, count, fresh):
        def some(base, start, fresh):
            at = pl.ds(base, count)
            where = pl.ds(column * line + start, span)
            q = queries[at].reshape(count * half, head_size)
            scores = dot_t(q, keys[where].reshape(span * rows, head_size))
            ranks = [
                rank_of(lax.rem(spot + start + index, line) * pair + column)
                for index in range(span)
            ]
            joined = []
            for block in range(count):
                rank = rank_of(base + block)
                each = [
                    jnp.exp(
                        scores[block * half : (block + 1) * half, index * rows : (index + 1) * rows]
                        + jnp.where(ranks[index] <= rank, 0.0, -1e30)
                    )
                    for index in range(span)
                ]
                total = functools.reduce(jnp.add, each)
                totals[base + block] = total if fresh else totals[base + block] + total
                joined.append(jnp.concatenate([w.astype(BF16) for w in each], axis=1))
            product = dot(
                jnp.concatenate(joined, axis=0), values[where].reshape(span * rows, head_size)
            ).reshape(count, half, head_size)
            acc[at] = product if fresh else acc[at] + product

        pl.loop(0, line // span)(lambda index: some(base, index * span, False))

    def score(column):
        where = pl.ds(column * line, line)
        q = queries[...].reshape(n * half, head_size)
        scores = dot_t(q, keys[where].reshape(line * rows, head_size))
        ranks = [
            rank_of(lax.rem(spot + index, line) * pair + column) for index in range(line)
        ]
        for block in range(n):
            rank = rank_of(block)
            each = [
                jnp.exp(
                    scores[block * half : (block + 1) * half, index * rows : (index + 1) * rows]
                    + jnp.where(ranks[index] <= rank, 0.0, -1e30)
                )
                for index in range(line)
            ]
            total = functools.reduce(jnp.add, each)
            opening = column is core
            totals[block] = total if opening else totals[block] + total
            seen[1 - int(opening), block] = jnp.concatenate(
                [w.astype(BF16) for w in each], axis=1
            )

    def product(which, column, at, count):
        value = values[pl.ds(column * line, line)].reshape(line * rows, head_size)
        return dot(
            seen[which, at].reshape(count * half, line * rows), value
        ).reshape(count, half, head_size)


    @pl.when(active)
    def _():
        if not simple:
            acc[...] = jnp.zeros_like(acc)
            totals[...] = jnp.zeros_like(totals)

        @pl.when(local)
        def _():
            queries[me] = stage[0, own_head, pl.ds(pl.multiple_of(core * half, half), half)]
            for kind in range(2):
                kv[kind][lane * line] = stage[1 + kind, own_head]
            landed(queries.at[0 : n - 1], q_sem.at[1])

        @pl.when(jnp.logical_not(local))
        def _():
            landed(queries, q_sem.at[1])

        column_landed(0, 2, core)
        relay_on(0)
        other = 1 - core
        if simple:
            score(core)
        column_landed(0, 0, other)
        if simple:
            score(other)
        place = lax.rem(oldest, pair) * line + lax.rem(oldest // pair - spot + line, line)
        weights = jnp.exp(dot_t(queries[oldest], keys[place]))
        weight_sum = jnp.sum(weights, axis=-1, keepdims=True)
        values_landed()
        blocks = min(n, 8)
        if simple:
            acc[...] = product(0, core, slice(None), n)
        else:
            pl.loop(0, n // blocks)(lambda index: absorb(core, index * blocks, blocks, False))
        column_landed(1, 1, other)

        lead = dot(weights.astype(BF16), values[place])
        lead = (lead / weight_sum).astype(BF16)

        def slab_fill(block):
            at = lax.rem(slab_of(block), half)
            chosen = lead[0:slab]
            for index in range(1, half // slab):
                chosen = jnp.where(
                    jnp.full((slab, head_size), at, jnp.int32) == index * slab,
                    lead[index * slab : (index + 1) * slab], chosen,
                )
            result[block, half:] = chosen

        batch = min(n // 2, 4)

        def batch_at(step):
            return jnp.where(me < n // 2, n // batch - 1 - step, step) * batch

        def last(step):
            base = batch_at(step)
            at = pl.ds(base, batch)
            if simple:
                value = acc[at] + product(1, other, at, batch)
            else:
                absorb(other, base, batch, False)
                value = acc[at]
            for index in range(batch):
                block = base + index
                total = jnp.sum(totals[block], axis=-1, keepdims=True)
                result[block, 0:half] = (value[index] / total).astype(BF16)
                slab_fill(block)
            for index in range(batch):
                target = base + index

                @pl.when(target != me)
                def _():
                    back_copy(target).start()

        if n == 2 * batch:
            last(0)
            last(1)
        else:
            pl.loop(0, n // batch)(last)
        attended[slot_at, own_head, own_piece] = result[me]

    def region(slot, h):
        return attended.at[slot, h, own_piece]

    def to_sibling(slot, h, kind):
        held = region(slot, h)
        return remote(
            held, held, pass_send.at[0], sib_recv.at[kind], {"tensor": sibling}
        )

    def across(slot, h, g, step):
        held = region(slot, h)
        return remote(
            held, held, pass_send.at[1], cross_recv.at[step - 1, g],
            {"tensor": lax.rem(plane + step, planes) * pair + core},
        )

    def ordered(step):
        g = jnp.where(me < n // 2, owners - 1 - step, step)
        return g, plane * pair + lax.rem(g, pair), g // pair

    def row_copy(target_spot):
        return remote(
            mixed_rows.at[target_spot], clean_rows_ref.at[spot], row_sem.at[2], row_sem.at[3],
            {"seq": target_spot * pair + lane},
        )

    def share_rows():
        landed(lat_rows, row_sem.at[1])
        swapped = jnp.full((slab, columns), buddy, jnp.int32) == oldest
        for step in range(line):
            target = step * pair + lane
            kept = lat[pl.ds(slab_of(target), slab), pl.ds(first_column, columns)]
            mixed_rows[step] = jnp.where(swapped, lat_rows[step], kept)
        clean_rows_ref[spot] = mixed_rows[spot]


        @pl.loop(1, line)
        def _(step):
            row_copy(lax.rem(spot + step, line)).start()

        @pl.loop(1, n)
        def _(step):
            gate_copy(lax.rem(me + step, n)).start()


    @pl.when(active)
    def _():
        for way in range(1, planes):
            across(slot_at, own_head, mine, way).start()
        to_sibling(slot_at, own_head, 0).start()

    share_rows()
    for step in range(owners):
        g, slot, h = ordered(step)

        @pl.when(first + g != me)
        def _():
            landed(region(slot, h), direct_recv.at[g])
            for way in range(1, planes):
                across(slot, h, g, way).start()
            to_sibling(slot, h, 0).start()

    def plane_dot(base, span):
        joined = jnp.concatenate(
            [attended[base + which, h, span] for which in range(pair) for h in range(heads)],
            axis=1,
        )
        weights = wout[pl.ds(base, pair)].reshape(pair * inner, columns)
        return dot(joined, weights)

    def finish(which):
        start = pl.multiple_of(which * piece, 16)
        total = partial[pl.ds(start, piece), :]
        for way in range(1, planes):
            base = lax.rem(plane + way, planes) * pair
            total = total + plane_dot(base, pl.ds(start, piece))
        at = pl.ds(pl.multiple_of(which * half, half), half)
        states = lat[at, pl.ds(first_column, columns)].astype(F32)
        updated = (states + gates[me] * total[0:half]).astype(BF16)
        leaving = jnp.full((half, columns), rank_of(me), jnp.int32) == 0
        updated_ref[at, :] = jnp.where(leaving, noise[at, :], updated)

        @pl.when(own_slab // half == which)
        def _():
            updated_ref[rows:, :] = (
                clean_rows_ref[oldest // pair].astype(F32) + gates[oldest] * total[half:]
            ).astype(BF16)

    for way in range(1, planes):
        for step in range(owners):
            g, slot, h = ordered(step)
            slot = lax.rem(slot + (planes - way) * pair, parts)
            landed(region(slot, h), cross_recv.at[way - 1, g])
            to_sibling(slot, h, 1).start()

    loads[8].wait()
    landed(wout.at[0], w_recv.at[2])
    landed(attended.at[0:pair, :, 0:piece], sib_recv.at[0])
    partial[...] = plane_dot(plane * pair, slice(None))
    landed(wout.at[0 : parts - pair, always], w_recv.at[1])
    landed(wout.at[0 : parts - pair, 0:third], w_recv.at[3])
    landed(gates.at[0 : n - 1], gate_sem.at[1])
    landed(lat_rows.at[0 : line - 1], row_sem.at[3])
    loads[9].wait()
    finish(core)
    landed(attended.at[0 : parts - pair, :, 0:piece], sib_recv.at[1])
    finish(1 - core)

    sent(mods.at[0 : parts - 1], mod_send.at[0])

    @pl.when(active & local)
    def _():
        sent(queries.at[0 : owners - 1], q_sem.at[0])

    @pl.when(jnp.logical_not(active & local))
    def _():
        sent(queries.at[0:owners], q_sem.at[0])

    sent(keys.at[0 : pair * heads], kv_send.at[0])
    sent(gates.at[0 : n - 1], gate_sem.at[0])
    sent(lat_rows, row_sem.at[0])
    sent(lat_rows.at[0 : line - 1], row_sem.at[2])
    sent(wout.at[0 : parts - pair, 0 : inner - third], w_send.at[0])
    sent(wout.at[0], w_send.at[1])
    sent(wout.at[0 : parts - pair, 0:third], w_send.at[2])
    sent(attended.at[:, :, 0:piece], pass_send.at[0])
    sent(attended.at[0 : parts - pair, :, 0:piece], pass_send.at[1])

    @pl.when(active)
    def _():
        sent(result.at[0 : n - 1], back_send.at[0])

        @pl.when(core == lane)
        def _():
            sent(keys.at[0 : pair * (line - 1)], relay_send.at[0])

        @pl.when(core != lane)
        def _():
            sent(keys, relay_send.at[0])


def finish_kernel(updated_ref, window_ref, clean_ref):
    rows = window_ref.shape[0]
    window_ref[...] = updated_ref[0:rows, :]
    clean_ref[...] = updated_ref[rows:, :]


def local(
    latents, levels, head_slot, fresh_noise, ada_weight, qkv_weight, q_gain, k_gain, out_weight
):
    n = lax.axis_size("seq")
    parts = lax.axis_size("tensor")
    rows, width = latents.shape
    columns = fresh_noise.shape[1]
    inner = out_weight.shape[0]
    clean_rows = rows // n
    slab = max(clean_rows, 16)
    heads = inner // q_gain.shape[0]
    head_size = q_gain.shape[0]
    half = rows // 2
    owners = 2 * heads
    vmem = pl.BlockSpec(memory_space=pltpu.VMEM)
    smem = pl.BlockSpec(memory_space=pltpu.SMEM)
    hbm = pl.BlockSpec(memory_space=pltpu.HBM)
    dma = pltpu.SemaphoreType.DMA
    updated = pl.pallas_call(
        functools.partial(kernel, n, parts, slab, clean_rows),
        out_shape=pltpu.VMEM((rows + slab, columns), BF16),
        in_specs=[
            smem, smem, hbm, hbm, hbm, hbm, hbm, hbm, hbm,
        ],
        out_specs=vmem,
        scratch_shapes=[
            pltpu.VMEM((2, 1, head_size), F32),
            pltpu.VMEM((rows, columns), BF16),
            pltpu.VMEM((rows, width), BF16),
            pltpu.VMEM((3, ada_weight.shape[0], columns), BF16),
            pltpu.VMEM((3, parts, columns, inner), BF16),
            pltpu.VMEM((parts, inner, columns), BF16),
            pltpu.VMEM((parts, rows, columns), F32),
            pltpu.VMEM((parts, 2, columns), F32),
            pltpu.VMEM((n, 1, columns), F32),
            pltpu.VMEM((n // 2, slab, columns), BF16),
            pltpu.VMEM((n // 2, slab, columns), BF16),
            pltpu.VMEM((n // 2, slab, columns), BF16),
            pltpu.VMEM((3, rows, inner), F32),
            pltpu.VMEM((3, heads, rows, head_size), BF16),
            pltpu.VMEM((n, half, head_size), BF16),
            pltpu.VMEM((n, rows, head_size), BF16),
            pltpu.VMEM((n, rows, head_size), BF16),
            pltpu.VMEM((n, half, head_size), F32),
            pltpu.VMEM((n, half, rows), F32),
            pltpu.VMEM((2, n if n <= 8 else 1, half, n // 2 * rows), BF16),
            pltpu.VMEM((n, half + slab, head_size), BF16),
            pltpu.VMEM((parts, heads, 2 * (half + slab), head_size), BF16),
            pltpu.VMEM((2 * (half + slab), columns), F32),
            pltpu.SemaphoreType.REGULAR, dma((10,)), dma((1,)), dma((2,)), dma((2,)), dma((4,)), dma((3,)), dma((4 + parts - 2,)),
            dma((2,)), dma((1,)), dma((3 + n // 2,)), dma((1,)), dma((1,)), dma((owners,)),
            dma((parts // 2 - 1, owners)), dma((2,)), dma((2,)),
        ],
        compiler_params=pltpu.CompilerParams(
            collective_id=0, has_side_effects=True, vmem_limit_bytes=60 * 1024 * 1024
        ),
    )(
        head_slot, levels, q_gain.reshape(1, -1), k_gain.reshape(1, -1), fresh_noise, latents,
        jnp.transpose(ada_weight, (1, 0, 2)),
        jnp.transpose(qkv_weight, (1, 0, 2)).reshape(3, parts, columns, inner), out_weight,
    )
    updated = pltpu.with_memory_space_constraint(updated, pltpu.VMEM)
    window, clean = pl.pallas_call(
        finish_kernel,
        out_shape=(
            jax.ShapeDtypeStruct((rows, columns), BF16),
            jax.ShapeDtypeStruct((slab, columns), BF16),
        ),
        in_specs=[vmem],
        out_specs=(vmem, vmem),
    )(updated)
    if clean_rows < slab:
        start = (lax.axis_index("seq") * clean_rows) % slab
        clean = lax.dynamic_slice_in_dim(clean, start, clean_rows, 0)
    return window, clean


def solution(mesh):
    return jax.shard_map(
        local,
        mesh=mesh,
        in_specs=(
            P("seq", None),
            P("seq"),
            P(),
            P(None, "tensor"),
            P(None, None, "tensor"),
            P(None, None, "tensor"),
            P(),
            P(),
            P("tensor", None),
        ),
        out_specs=(P("seq", "tensor"), P("seq", "tensor")),
        check_vma=False,
    )
```

```python
import functools
import math

import jax
import jax.numpy as jnp
from jax import lax
from jax.experimental import pallas as pl
from jax.experimental.pallas import tpu as pltpu
from jax.sharding import PartitionSpec as P

F32 = jnp.float32
BF16 = jnp.bfloat16
EPS = 1e-06


def dot(a, b):
    return jnp.dot(a, b, preferred_element_type=F32)


def dot_t(a, b):
    return lax.dot_general(a, b, (((1,), (1,)), ((), ())), preferred_element_type=F32)


def kernel(
    n, parts, slab, clean_rows,
    head_ref, level_ref, q_gain_hbm, k_gain_hbm, noise_hbm, lat_hbm, ada_hbm, qkv_hbm, out_hbm,
    updated_ref,
    gains, noise, lat, ada, wqkv, wout, normed, mods, gates,
    lat_rows, mixed_rows, clean_rows_ref, raw, stage, queries, keys, values, acc, totals, seen, result, attended, partial,
    ready, load_sem, mod_send, mod_recv, gate_sem, row_sem, w_send, w_recv,
    q_sem, kv_send, kv_recv, relay_send, back_send, direct_recv, cross_recv, sib_recv, pass_send,
):
    kv = (keys, values)
    me = lax.axis_index("seq")
    part = lax.axis_index("tensor")
    pair = 2
    core = lax.rem(part, pair)
    plane = part // pair
    planes = parts // pair
    sibling = plane * pair + 1 - core
    lane = lax.rem(me, pair)
    spot = me // pair
    line = n // pair
    buddy = me + 1 - pair * lane
    rows, width = lat.shape
    columns = updated_ref.shape[1]
    inner = wout.shape[1]
    head_size = gains.shape[2]
    heads = stage.shape[1]
    half = rows // pair
    piece = half + slab
    owners = heads * pair
    first = (n - owners) // 2
    mine = me - first
    active = (mine >= 0) & (mine < owners)
    own_head = jnp.clip(mine // pair, 0, heads - 1)
    own_core = lax.rem(mine + owners * n, pair)
    local = own_core == core
    others = [
        lax.rem(plane + step, planes) * pair + lax.rem(core + which, pair)
        for step in range(1, planes) for which in range(pair)
    ]

    def remote(src, dst, send, recv, target):
        return pltpu.make_async_remote_copy(
            src_ref=src, dst_ref=dst, send_sem=send, recv_sem=recv,
            device_id=target, device_id_type=pl.DeviceIdType.MESH,
        )

    def landed(ref, sem):
        remote(ref, ref, sem, sem, {"tensor": sibling}).wait_recv()

    def sent(ref, sem):
        remote(ref, ref, sem, sem, {"tensor": sibling}).wait_send()

    def at_core(seq, which):
        return {"seq": seq, "tensor": plane * pair + which}

    loads = [
        pltpu.make_async_copy(ada_hbm.at[0:2], ada.at[0:2], load_sem.at[0]),
        pltpu.make_async_copy(lat_hbm, lat, load_sem.at[1]),
        pltpu.make_async_copy(qkv_hbm.at[0], wqkv.at[0], load_sem.at[2]),
        pltpu.make_async_copy(qkv_hbm.at[1], wqkv.at[1], load_sem.at[3]),
        pltpu.make_async_copy(qkv_hbm.at[2], wqkv.at[2], load_sem.at[4]),
        pltpu.make_async_copy(ada_hbm.at[2], ada.at[2], load_sem.at[5]),
        pltpu.make_async_copy(q_gain_hbm, gains.at[0], load_sem.at[6]),
        pltpu.make_async_copy(k_gain_hbm, gains.at[1], load_sem.at[7]),
        pltpu.make_async_copy(
            out_hbm.at[:, pl.ds(pl.multiple_of(part * columns, 128), columns)],
            wout.at[part], load_sem.at[8],
        ),
        pltpu.make_async_copy(noise_hbm, noise, load_sem.at[9]),
    ]
    barrier = pltpu.get_barrier_semaphore()

    loads[0].start()
    for step in range(planes):
        slot = lax.rem(plane + step, planes) * pair

        @pl.when(slot != part)
        def _():
            pl.semaphore_signal(
                barrier, inc=1, device_id={"tensor": slot}, device_id_type=pl.DeviceIdType.MESH
            )

    for load in loads[1:5]:
        load.start()

    @pl.loop(1, n)
    def _(step):
        pl.semaphore_signal(
            barrier, inc=1, device_id=at_core(lax.rem(me + step, n), pair - 1),
            device_id_type=pl.DeviceIdType.MESH,
        )


    half_width = ada.shape[1] // 2
    order = lax.broadcasted_iota(jnp.int32, (16, half_width), 1).astype(F32)
    angles = level_ref[0].astype(F32) * jnp.exp(-math.log(10000.0) * order / half_width)
    waves = jnp.concatenate([jnp.cos(angles), jnp.sin(angles)], axis=1)
    emb = (waves * (1.0 / (1.0 + jnp.exp(-waves)))).astype(BF16)
    def tell_sibling():
        pl.semaphore_signal(
            ready, inc=1, device_id={"tensor": sibling}, device_id_type=pl.DeviceIdType.MESH
        )

    @pl.when(core == 0)
    def _():
        pl.semaphore_wait(barrier, parts - 1)
        tell_sibling()

    @pl.when(core != 0)
    def _():
        pl.semaphore_wait(ready, 1)

    loads[0].wait()
    for j in range(2):
        mods[part, j : j + 1, :] = dot(emb, ada[j])[0:1]

    def meet():
        @pl.when(core != 0)
        def _():
            pl.semaphore_wait(barrier, pair * (n - 1))
            tell_sibling()

        @pl.when(core == 0)
        def _():
            pl.semaphore_wait(ready, 1)


    def mod_copy(target, near):
        return remote(
            mods.at[part], mods.at[part], mod_send.at[0], mod_recv.at[near], {"tensor": target}
        )

    for slot in others:
        mod_copy(slot, 1).start()
    mod_copy(sibling, 0).start()

    third = inner // 3 // 16 * 16
    own_third = pl.ds(pl.multiple_of(inner - (pair - lane) * third, 16), third)
    always = pl.ds(0, inner - pair * third)

    def w_copy(target, span, send, recv):
        at = pl.ds(pl.multiple_of(target * columns, 128), columns)
        return remote(
            out_hbm.at[span, at], wout.at[part, span], w_send.at[send], w_recv.at[recv],
            {"tensor": target},
        )

    for index, slot in enumerate(others):
        w_copy(slot, own_third, 0, 4 + index).start()
    for slot in others:
        w_copy(slot, always, 0, 1).start()

    def slab_of(device):
        return pl.multiple_of((device * clean_rows) // slab * slab, slab)

    first_column = pl.multiple_of(part * columns, 128)

    def swap_copy(step):
        return remote(
            lat_hbm.at[pl.ds(slab_of(step * pair + 1 - lane), slab), pl.ds(first_column, columns)],
            lat_rows.at[step], row_sem.at[0], row_sem.at[1], {"seq": buddy},
        )

    def gate_copy(target):
        return remote(
            gates.at[me], gates.at[me], gate_sem.at[0], gate_sem.at[1], {"seq": target}
        )

    loads[1].wait()
    own_slab = slab_of(me)

    tile = 16

    @pl.loop(0, rows // tile, unroll=4)
    def _(index):
        at = pl.ds(pl.multiple_of(index * tile, tile), tile)
        states = lat[at, :].astype(F32)
        centered = states - jnp.mean(states, axis=-1, keepdims=True)
        variance = jnp.mean(centered * centered, axis=-1, keepdims=True)
        scaled_rows = centered * lax.rsqrt(variance + EPS)
        for index in range(parts):
            normed[index, at, :] = scaled_rows[:, index * columns : (index + 1) * columns]

    def hidden_of(slot):
        return (normed[slot] * (1.0 + mods[slot, 1:2, :]) + mods[slot, 0:1, :]).astype(BF16)

    own_hidden = hidden_of(part)
    for kind in range(3):
        loads[2 + kind].wait()
        raw[kind] = dot(own_hidden, wqkv[kind, part])
    for load in loads[5:]:
        load.start()
    landed(mods.at[0], mod_recv.at[0])
    sib_hidden = hidden_of(sibling)
    for kind in range(3):
        raw[kind] += dot(sib_hidden, wqkv[kind, sibling])

    loads[6].wait()
    loads[7].wait()
    landed(mods.at[0 : parts - pair], mod_recv.at[1])
    rest = [hidden_of(slot) for slot in others]

    def whole(kind):
        total = raw[kind]
        for hidden, slot in zip(rest, others):
            total = total + dot(hidden, wqkv[kind, slot])
        return total

    def scaled(matrix, gain, factor):
        power = jnp.mean(matrix * matrix, axis=-1, keepdims=True)
        return (matrix * lax.rsqrt(power + EPS) * gain * factor).astype(BF16)

    def head_at(index):
        return slice(index * head_size, (index + 1) * head_size)

    def turn(step):
        return jnp.where(me < n // 2, heads - 1 - step, step)

    def owner_of(h):
        return first + pair * h + core

    def send(kind, step):
        h = turn(step)
        owner = owner_of(h)
        if kind == 0:
            for which in range(pair):

                @pl.when((owner != me) | (core != which))
                def _():
                    remote(
                        stage.at[0, h, pl.ds(which * half, half)], queries.at[me],
                        q_sem.at[0], q_sem.at[1], at_core(owner, which),
                    ).start()
        else:
            which = jnp.where(owner == me, 1 - core, lane)
            relayed = jnp.where(which == lane, 0, 1)
            place = lane * line + lax.rem(spot - owner // pair + line, line)
            remote(
                stage.at[kind, h], kv[kind - 1].at[place], kv_send.at[0],
                kv_recv.at[jnp.where(relayed == 1, kind - 1, 2 if kind == 1 else 3 + place - lane * line)],
                at_core(owner, which),
            ).start()

    def send_all(kind):
        for step in range(heads):
            send(kind, step)

    value = whole(2)
    for h in range(heads):
        stage[2, h] = value[:, head_at(h)].astype(BF16)
    meet()
    send_all(2)
    value = whole(1)
    for h in range(heads):
        stage[1, h] = scaled(value[:, head_at(h)], gains[1], 1.0)
    send_all(1)
    value = whole(0)
    for h in range(heads):
        stage[0, h] = scaled(value[:, head_at(h)], gains[0], 1.0 / math.sqrt(head_size))
    send_all(0)

    w_copy(sibling, pl.ds(0, inner), 1, 2).start()

    @pl.loop(0, line)
    def _(step):
        swap_copy(step).start()

    oldest = head_ref[0]
    loads[5].wait()
    gates[me] = dot(emb, ada[2])[0:1]
    for index, slot in enumerate(others):
        held = wout.at[slot, own_third]
        landed(held, w_recv.at[4 + index])
        remote(held, held, w_send.at[2], w_recv.at[3], {"seq": buddy}).start()

    def rank_of(block):
        return lax.rem(block - oldest + n, n)

    def column_landed(kind, sem, column):
        @pl.when(local & (column == lane))
        def _():
            landed(kv[kind].at[0 : line - 1], kv_recv.at[sem])

        @pl.when(jnp.logical_not(local & (column == lane)))
        def _():
            landed(kv[kind].at[0:line], kv_recv.at[sem])

    def relay(kind, skip):
        held = kv[kind].at[pl.ds(core * line + skip, line - skip)]
        return remote(held, held, relay_send.at[0], kv_recv.at[kind], {"tensor": sibling})

    def values_landed():
        @pl.loop(0, line)
        def _(place):
            held = values.at[core * line + place]
            inside = (place == 0) & (core == lane)

            @pl.when(jnp.logical_not(inside & local))
            def _():
                landed(held, kv_recv.at[3 + place])

            @pl.when(jnp.logical_not(inside))
            def _():
                remote(
                    held, held, relay_send.at[0], kv_recv.at[1], {"tensor": sibling}
                ).start()

    def relay_on(kind):
        @pl.when(core == lane)
        def _():
            relay(kind, 1).start()

        @pl.when(core != lane)
        def _():
            relay(kind, 0).start()

    slot_at = plane * pair + own_core
    own_piece = pl.ds(pl.multiple_of(core * piece, 16), piece)

    def back_copy(target):
        return remote(
            result.at[target], attended.at[slot_at, own_head, own_piece],
            back_send.at[0], direct_recv.at[own_head * pair + own_core], at_core(target, core),
        )

    span = min(line, 4)
    simple = line == span

    def absorb(column, base, count, fresh):
        def some(base, start, fresh):
            at = pl.ds(base, count)
            where = pl.ds(column * line + start, span)
            q = queries[at].reshape(count * half, head_size)
            scores = dot_t(q, keys[where].reshape(span * rows, head_size))
            ranks = [
                rank_of(lax.rem(spot + start + index, line) * pair + column)
                for index in range(span)
            ]
            joined = []
            for block in range(count):
                rank = rank_of(base + block)
                each = [
                    jnp.exp(
                        scores[block * half : (block + 1) * half, index * rows : (index + 1) * rows]
                        + jnp.where(ranks[index] <= rank, 0.0, -1e30)
                    )
                    for index in range(span)
                ]
                total = functools.reduce(jnp.add, each)
                totals[base + block] = total if fresh else totals[base + block] + total
                joined.append(jnp.concatenate([w.astype(BF16) for w in each], axis=1))
            product = dot(
                jnp.concatenate(joined, axis=0), values[where].reshape(span * rows, head_size)
            ).reshape(count, half, head_size)
            acc[at] = product if fresh else acc[at] + product

        pl.loop(0, line // span)(lambda index: some(base, index * span, False))

    def score(column, base, count):
        where = pl.ds(column * line, line)
        q = queries[pl.ds(base, count)].reshape(count * half, head_size)
        scores = dot_t(q, keys[where].reshape(line * rows, head_size))
        ranks = [
            rank_of(lax.rem(spot + index, line) * pair + column) for index in range(line)
        ]
        for block in range(count):
            rank = rank_of(base + block)
            each = [
                jnp.exp(
                    scores[block * half : (block + 1) * half, index * rows : (index + 1) * rows]
                    + jnp.where(ranks[index] <= rank, 0.0, -1e30)
                )
                for index in range(line)
            ]
            total = functools.reduce(jnp.add, each)
            opening = column is core
            totals[base + block] = total if opening else totals[base + block] + total
            seen[1 - int(opening), base + block] = jnp.concatenate(
                [w.astype(BF16) for w in each], axis=1
            )

    def product(which, column, at, count):
        value = values[pl.ds(column * line, line)].reshape(line * rows, head_size)
        return dot(
            seen[which, at].reshape(count * half, line * rows), value
        ).reshape(count, half, head_size)


    @pl.when(active)
    def _():
        if not simple:
            acc[...] = jnp.zeros_like(acc)
            totals[...] = jnp.zeros_like(totals)

        @pl.when(local)
        def _():
            queries[me] = stage[0, own_head, pl.ds(pl.multiple_of(core * half, half), half)]
            for kind in range(2):
                kv[kind][lane * line] = stage[1 + kind, own_head]

        other = 1 - core
        values_landed()
        column_landed(0, 2, core)
        relay_on(0)
        column_landed(0, 0, other)
        column_landed(1, 1, other)

        @pl.when(local)
        def _():
            landed(queries.at[0 : n - 1], q_sem.at[1])

        @pl.when(jnp.logical_not(local))
        def _():
            landed(queries, q_sem.at[1])

        place = lax.rem(oldest, pair) * line + lax.rem(oldest // pair - spot + line, line)
        weights = jnp.exp(dot_t(queries[oldest], keys[place]))
        weight_sum = jnp.sum(weights, axis=-1, keepdims=True)
        blocks = min(n, 8)
        if not simple:
            pl.loop(0, n // blocks)(lambda index: absorb(core, index * blocks, blocks, False))

        lead = dot(weights.astype(BF16), values[place])
        lead = (lead / weight_sum).astype(BF16)

        def slab_fill(block):
            at = lax.rem(slab_of(block), half)
            chosen = lead[0:slab]
            for index in range(1, half // slab):
                chosen = jnp.where(
                    jnp.full((slab, head_size), at, jnp.int32) == index * slab,
                    lead[index * slab : (index + 1) * slab], chosen,
                )
            result[block, half:] = chosen

        batch = min(n // 2, 4)

        def batch_at(step):
            return jnp.where(me < n // 2, n // batch - 1 - step, step) * batch

        def last(step):
            base = batch_at(step)
            at = pl.ds(base, batch)
            if simple:
                score(core, base, batch)
                score(other, base, batch)
                value = product(0, core, at, batch) + product(1, other, at, batch)
            else:
                absorb(other, base, batch, False)
                value = acc[at]
            for index in range(batch):
                block = base + index
                total = jnp.sum(totals[block], axis=-1, keepdims=True)
                result[block, 0:half] = (value[index] / total).astype(BF16)
                slab_fill(block)
            for index in range(batch):
                target = base + index

                @pl.when(target != me)
                def _():
                    back_copy(target).start()

        if n == 2 * batch:
            last(0)
            last(1)
        else:
            pl.loop(0, n // batch)(last)
        attended[slot_at, own_head, own_piece] = result[me]

    def region(slot, h):
        return attended.at[slot, h, own_piece]

    def to_sibling(slot, h, kind):
        held = region(slot, h)
        return remote(
            held, held, pass_send.at[0], sib_recv.at[kind], {"tensor": sibling}
        )

    def across(slot, h, g, step):
        held = region(slot, h)
        return remote(
            held, held, pass_send.at[1], cross_recv.at[step - 1, g],
            {"tensor": lax.rem(plane + step, planes) * pair + core},
        )

    def ordered(step):
        g = jnp.where(me < n // 2, owners - 1 - step, step)
        return g, plane * pair + lax.rem(g, pair), g // pair

    def row_copy(target_spot):
        return remote(
            mixed_rows.at[target_spot], clean_rows_ref.at[spot], row_sem.at[2], row_sem.at[3],
            {"seq": target_spot * pair + lane},
        )

    def share_rows():
        landed(lat_rows, row_sem.at[1])
        swapped = jnp.full((slab, columns), buddy, jnp.int32) == oldest
        for step in range(line):
            target = step * pair + lane
            kept = lat[pl.ds(slab_of(target), slab), pl.ds(first_column, columns)]
            mixed_rows[step] = jnp.where(swapped, lat_rows[step], kept)
        clean_rows_ref[spot] = mixed_rows[spot]


        @pl.loop(1, line)
        def _(step):
            row_copy(lax.rem(spot + step, line)).start()

        @pl.loop(1, n)
        def _(step):
            gate_copy(lax.rem(me + step, n)).start()


    @pl.when(active)
    def _():
        for way in range(1, planes):
            across(slot_at, own_head, mine, way).start()
        to_sibling(slot_at, own_head, 0).start()

    share_rows()
    for step in range(owners):
        g, slot, h = ordered(step)

        @pl.when(first + g != me)
        def _():
            landed(region(slot, h), direct_recv.at[g])
            for way in range(1, planes):
                across(slot, h, g, way).start()
            to_sibling(slot, h, 0).start()

    def plane_dot(base, span):
        joined = jnp.concatenate(
            [attended[base + which, h, span] for which in range(pair) for h in range(heads)],
            axis=1,
        )
        weights = wout[pl.ds(base, pair)].reshape(pair * inner, columns)
        return dot(joined, weights)

    def finish(which):
        start = pl.multiple_of(which * piece, 16)
        total = partial[pl.ds(start, piece), :]
        for way in range(1, planes):
            base = lax.rem(plane + way, planes) * pair
            total = total + plane_dot(base, pl.ds(start, piece))
        at = pl.ds(pl.multiple_of(which * half, half), half)
        states = lat[at, pl.ds(first_column, columns)].astype(F32)
        updated = (states + gates[me] * total[0:half]).astype(BF16)
        leaving = jnp.full((half, columns), rank_of(me), jnp.int32) == 0
        updated_ref[at, :] = jnp.where(leaving, noise[at, :], updated)

        @pl.when(own_slab // half == which)
        def _():
            updated_ref[rows:, :] = (
                clean_rows_ref[oldest // pair].astype(F32) + gates[oldest] * total[half:]
            ).astype(BF16)

    for way in range(1, planes):
        for step in range(owners):
            g, slot, h = ordered(step)
            slot = lax.rem(slot + (planes - way) * pair, parts)
            landed(region(slot, h), cross_recv.at[way - 1, g])
            to_sibling(slot, h, 1).start()

    loads[8].wait()
    landed(wout.at[0], w_recv.at[2])
    landed(attended.at[0:pair, :, 0:piece], sib_recv.at[0])
    partial[...] = plane_dot(plane * pair, slice(None))
    landed(wout.at[0 : parts - pair, always], w_recv.at[1])
    landed(wout.at[0 : parts - pair, 0:third], w_recv.at[3])
    landed(gates.at[0 : n - 1], gate_sem.at[1])
    landed(lat_rows.at[0 : line - 1], row_sem.at[3])
    loads[9].wait()
    finish(core)
    landed(attended.at[0 : parts - pair, :, 0:piece], sib_recv.at[1])
    finish(1 - core)

    sent(mods.at[0 : parts - 1], mod_send.at[0])

    @pl.when(active & local)
    def _():
        sent(queries.at[0 : owners - 1], q_sem.at[0])

    @pl.when(jnp.logical_not(active & local))
    def _():
        sent(queries.at[0:owners], q_sem.at[0])

    sent(keys.at[0 : pair * heads], kv_send.at[0])
    sent(gates.at[0 : n - 1], gate_sem.at[0])
    sent(lat_rows, row_sem.at[0])
    sent(lat_rows.at[0 : line - 1], row_sem.at[2])
    sent(wout.at[0 : parts - pair, 0 : inner - third], w_send.at[0])
    sent(wout.at[0], w_send.at[1])
    sent(wout.at[0 : parts - pair, 0:third], w_send.at[2])
    sent(attended.at[:, :, 0:piece], pass_send.at[0])
    sent(attended.at[0 : parts - pair, :, 0:piece], pass_send.at[1])

    @pl.when(active)
    def _():
        sent(result.at[0 : n - 1], back_send.at[0])

        @pl.when(core == lane)
        def _():
            sent(keys.at[0 : pair * (line - 1)], relay_send.at[0])

        @pl.when(core != lane)
        def _():
            sent(keys, relay_send.at[0])


def finish_kernel(updated_ref, window_ref, clean_ref):
    rows = window_ref.shape[0]
    window_ref[...] = updated_ref[0:rows, :]
    clean_ref[...] = updated_ref[rows:, :]


def local(
    latents, levels, head_slot, fresh_noise, ada_weight, qkv_weight, q_gain, k_gain, out_weight
):
    n = lax.axis_size("seq")
    parts = lax.axis_size("tensor")
    rows, width = latents.shape
    columns = fresh_noise.shape[1]
    inner = out_weight.shape[0]
    clean_rows = rows // n
    slab = max(clean_rows, 16)
    heads = inner // q_gain.shape[0]
    head_size = q_gain.shape[0]
    half = rows // 2
    owners = 2 * heads
    vmem = pl.BlockSpec(memory_space=pltpu.VMEM)
    smem = pl.BlockSpec(memory_space=pltpu.SMEM)
    hbm = pl.BlockSpec(memory_space=pltpu.HBM)
    dma = pltpu.SemaphoreType.DMA
    updated = pl.pallas_call(
        functools.partial(kernel, n, parts, slab, clean_rows),
        out_shape=pltpu.VMEM((rows + slab, columns), BF16),
        in_specs=[
            smem, smem, hbm, hbm, hbm, hbm, hbm, hbm, hbm,
        ],
        out_specs=vmem,
        scratch_shapes=[
            pltpu.VMEM((2, 1, head_size), F32),
            pltpu.VMEM((rows, columns), BF16),
            pltpu.VMEM((rows, width), BF16),
            pltpu.VMEM((3, ada_weight.shape[0], columns), BF16),
            pltpu.VMEM((3, parts, columns, inner), BF16),
            pltpu.VMEM((parts, inner, columns), BF16),
            pltpu.VMEM((parts, rows, columns), F32),
            pltpu.VMEM((parts, 2, columns), F32),
            pltpu.VMEM((n, 1, columns), F32),
            pltpu.VMEM((n // 2, slab, columns), BF16),
            pltpu.VMEM((n // 2, slab, columns), BF16),
            pltpu.VMEM((n // 2, slab, columns), BF16),
            pltpu.VMEM((3, rows, inner), F32),
            pltpu.VMEM((3, heads, rows, head_size), BF16),
            pltpu.VMEM((n, half, head_size), BF16),
            pltpu.VMEM((n, rows, head_size), BF16),
            pltpu.VMEM((n, rows, head_size), BF16),
            pltpu.VMEM((n, half, head_size), F32),
            pltpu.VMEM((n, half, rows), F32),
            pltpu.VMEM((2, n if n <= 8 else 1, half, n // 2 * rows), BF16),
            pltpu.VMEM((n, half + slab, head_size), BF16),
            pltpu.VMEM((parts, heads, 2 * (half + slab), head_size), BF16),
            pltpu.VMEM((2 * (half + slab), columns), F32),
            pltpu.SemaphoreType.REGULAR, dma((10,)), dma((1,)), dma((2,)), dma((2,)), dma((4,)), dma((3,)), dma((4 + parts - 2,)),
            dma((2,)), dma((1,)), dma((3 + n // 2,)), dma((1,)), dma((1,)), dma((owners,)),
            dma((parts // 2 - 1, owners)), dma((2,)), dma((2,)),
        ],
        compiler_params=pltpu.CompilerParams(
            collective_id=0, has_side_effects=True, vmem_limit_bytes=60 * 1024 * 1024
        ),
    )(
        head_slot, levels, q_gain.reshape(1, -1), k_gain.reshape(1, -1), fresh_noise, latents,
        jnp.transpose(ada_weight, (1, 0, 2)),
        jnp.transpose(qkv_weight, (1, 0, 2)).reshape(3, parts, columns, inner), out_weight,
    )
    updated = pltpu.with_memory_space_constraint(updated, pltpu.VMEM)
    window, clean = pl.pallas_call(
        finish_kernel,
        out_shape=(
            jax.ShapeDtypeStruct((rows, columns), BF16),
            jax.ShapeDtypeStruct((slab, columns), BF16),
        ),
        in_specs=[vmem],
        out_specs=(vmem, vmem),
    )(updated)
    if clean_rows < slab:
        start = (lax.axis_index("seq") * clean_rows) % slab
        clean = lax.dynamic_slice_in_dim(clean, start, clean_rows, 0)
    return window, clean


def solution(mesh):
    return jax.shard_map(
        local,
        mesh=mesh,
        in_specs=(
            P("seq", None),
            P("seq"),
            P(),
            P(None, "tensor"),
            P(None, None, "tensor"),
            P(None, None, "tensor"),
            P(),
            P(),
            P("tensor", None),
        ),
        out_specs=(P("seq", "tensor"), P("seq", "tensor")),
        check_vma=False,
    )
```
